256 devices in a mesh: dp: 32 (over z, x_hi, core), tensor: 8 (over x_lo, y).
Axes of the slice: x: 4 (x_hi: 2, x_lo: 2; x = x_hi * 2 + x_lo), y: 4, z: 8, core: 2. Of those that a mesh axis runs over, the one named last changes fastest.
Arguments:
- hidden: bfloat16 [16384, 14336], P('dp', 'tensor'), may hold values from -76 to 76
- base_weight: bfloat16 [14336, 4096], P('tensor', 'dp'), may hold values from -0.046875 to 0.046875
- adapter_in: bfloat16 [256, 14336], P(None, 'tensor'), may hold values from -0.046875 to 0.046875
- adapter_out: bfloat16 [256, 4096], P(None, 'tensor'), may hold values from -0.375 to 0.375
- cotangent: bfloat16 [16384, 4096], P('dp', 'tensor'), may hold values from -0.046875 to 0.046875
Outputs:
- output: bfloat16 [16384, 4096], P('dp', 'tensor')
- grad_in: float32 [256, 14336], P('dp', 'tensor')
- grad_out: float32 [256, 4096], P('dp', 'tensor')
The draws below stay inside these ranges and needn't reach their ends.
All inputs are finite; a program needn't handle non-finite values.
Results may differ from the reference program's by a relative error of at most 0.0031.
Values may be sent and summed in bfloat16 or wider, within the bound.
A program may use at most 128 MiB of HBM per device.

```python
import math
import jax
import jax.numpy as jnp
from jax import lax

FF = 14336
DOUT = 4096
RANK = 256
TOKENS = 16384


def draw_hidden(key, part):
    keys = jax.random.split(key, 3)
    row_pos = jnp.arange(TOKENS, dtype=jnp.float32) / max(TOKENS - 1, 1)
    col_pos = jnp.arange(FF, dtype=jnp.float32) / max(FF - 1, 1)
    row_rand = jnp.exp(jax.random.uniform(keys[0], (TOKENS, 1), jnp.float32, math.log(0.3), math.log(1.5)))
    col_rand = jnp.exp(jax.random.uniform(keys[1], (1, FF), jnp.float32, math.log(0.7), math.log(1.4)))
    values = jax.random.truncated_normal(keys[2], -4.0, 4.0, (TOKENS, FF), jnp.float32)
    scaled = values * row_rand * col_rand * (1.0 + 2.0 * row_pos)[:, None] * (1.0 + 2.0 * col_pos)[None, :]
    return scaled.astype(jnp.bfloat16)


def level_of(rng, extent, shards, least, high):
    gain, own = 1.0, jax.random.fold_in(rng, 6)
    for dim, parts in shards:
        steps = jnp.exp(jax.random.uniform(jax.random.fold_in(own, dim), (parts,), jnp.float32, least / len(shards), high / len(shards)))
        gain = gain * jnp.repeat(steps, extent[dim] // parts).reshape([-1 if axis == dim else 1 for axis in range(len(extent))])
    return gain


def normal_values(key, extent, width, bound, pieces=(), kind=jnp.bfloat16):
    drawn = jax.random.normal(key, extent, jnp.float32) * width
    if len(pieces) > 0:
        drawn = level_of(key, extent, pieces, -0.22, 0.18) * drawn
    return jnp.clip(drawn, min=-bound, max=bound).astype(kind)


def setup_inputs(seed: int = 0) -> dict:
    splits = jax.random.split(jax.random.key(seed), 6)
    hidden = draw_hidden(jax.random.fold_in(splits[5], 71), 0)
    base_weight = normal_values(splits[1], (FF, DOUT), FF ** -0.5, 0.046875, ((0, 8), (1, 32)))
    adapter_in = normal_values(splits[2], (RANK, FF), FF ** -0.5, 0.046875, ((1, 8),))
    adapter_out = normal_values(splits[3], (RANK, DOUT), RANK ** -0.5, 0.375, ((1, 8),))
    cotangent = normal_values(splits[4], (TOKENS, DOUT), (1.0 / TOKENS ** 0.5), 0.046875, ((0, 32), (1, 8)))
    return {"hidden": hidden, "base_weight": base_weight, "adapter_in": adapter_in, "adapter_out": adapter_out, "cotangent": cotangent}


adapter_scale = 4.0
exp_rate = 0.25
tiny_eps = 1e-06

def inverse_sinh(value):
    return jnp.log(value + jnp.sqrt(1.0 + value * value))

def reference(hidden, base_weight, adapter_in, adapter_out, cotangent):
    contract_last = (((1,), (1,)), ((), ()))
    contract_first = (((0,), (0,)), ((), ()))
    square_sum = lax.optimization_barrier(jnp.sum(jnp.square(hidden.astype(jnp.float32)), axis=1))
    level = jnp.sqrt(square_sum / FF + tiny_eps)
    radius = exp_rate * level
    lift_factor = jnp.sinh(radius) / radius
    lorentz_raw = lax.dot_general(hidden, adapter_in, contract_last, preferred_element_type=jnp.float32)
    lorentz = lift_factor[:, None] * lorentz_raw
    norm_value = jnp.sqrt(lax.optimization_barrier(jnp.sum(lorentz * lorentz, axis=1)) + tiny_eps)
    phi_value = inverse_sinh(norm_value) / norm_value
    tangent = (phi_value[:, None] * lorentz).astype(jnp.bfloat16)
    base_sum = jnp.dot(hidden, base_weight, preferred_element_type=jnp.float32)
    adapter_term = jnp.dot(tangent, adapter_out, preferred_element_type=jnp.float32)
    output = (base_sum + adapter_scale * adapter_term).astype(jnp.bfloat16)
    grad_out = adapter_scale * lax.dot_general(tangent, cotangent, contract_first, preferred_element_type=jnp.float32)
    tangent_grad = adapter_scale * lax.dot_general(cotangent, adapter_out, contract_last, preferred_element_type=jnp.float32)
    inner_value = lax.optimization_barrier(jnp.sum(lorentz * tangent_grad, axis=1))
    coefficient = (1.0 / jnp.sqrt(1.0 + norm_value * norm_value) - phi_value) / (norm_value * norm_value)
    lorentz_grad = phi_value[:, None] * tangent_grad + (coefficient * inner_value)[:, None] * lorentz
    raw_grad = (lift_factor[:, None] * lorentz_grad).astype(jnp.bfloat16)
    grad_in = lax.dot_general(raw_grad, hidden, contract_first, preferred_element_type=jnp.float32)
    return (output, grad_in, grad_out)
```

```python
import functools

import jax
import jax.numpy as jnp
from jax import lax
from jax.experimental import pallas as pl
from jax.experimental.pallas import tpu as pltpu
from jax.sharding import PartitionSpec as P

adapter_scale = 4.0
exp_rate = 0.25
tiny_eps = 1e-06

MESH = pl.DeviceIdType.MESH
NZ, NY, NT = 8, 4, 8
F32, BF16 = jnp.float32, jnp.bfloat16
LAST = (((1,), (1,)), ((), ()))
FIRST = (((0,), (0,)), ((), ()))
LAG = 4


def lift_of(radius):
    sq = radius * radius
    series = 1.0 + sq / 6.0 * (
        1.0 + sq / 20.0 * (1.0 + sq / 42.0 * (1.0 + sq / 72.0 * (1.0 + sq / 110.0)))
    )
    direct = (jnp.exp(radius) - jnp.exp(-radius)) / (2.0 * radius)
    return jnp.where(radius < 1.0, series, direct)


def kernel(
    features,
    hid_hbm, b_hbm, ain_hbm, aout_hbm, cot_hbm,
    out_ref, gin_ref, gout_ref,
    hid, ain, aout, cot, weights, psend, precv, acc, xsend, xrecv,
    rsend, rrecv, td, gpart, g1recv, g2send, g2recv, g3send, g3recv, adapt,
    local_sem, bsend, bsend2, brecv, ssend, srecv, csend_sem, crecv_sem,
    xsend_sem, xrecv_sem, rsend_sem, rrecv_sem, asend_sem, arecv_sem,
    g12send_sem, g12recv_sem, g3send_sem, g3recv_sem,
):
    d, t = lax.axis_index("dp"), lax.axis_index("tensor")
    z, h, c = d // 4, (d // 2) % 2, d % 2
    xl, y = t // NY, t % NY
    tokens = hid.shape[0]

    def at(z_, h_, c_):
        return (z_ * 4 + h_ * 2 + c_, t)

    zup, zdown = at((z + 1) % NZ, h, c), at((z + NZ - 1) % NZ, h, c)
    partner, sibling = at(z, 1 - h, c), at(z, h, 1 - c)

    loads = [
        pltpu.make_async_copy(b_hbm, weights.at[z, h, c], local_sem.at[0]),
        pltpu.make_async_copy(hid_hbm, hid, local_sem.at[1]),
        pltpu.make_async_copy(ain_hbm, ain, local_sem.at[2]),
        pltpu.make_async_copy(cot_hbm, cot, local_sem.at[3]),
        pltpu.make_async_copy(aout_hbm, aout, local_sem.at[4]),
    ]
    for load in loads:
        load.start()

    barrier = pltpu.get_barrier_semaphore()
    peers = [at((z + i) % NZ, h, c) for i in range(1, NZ)]
    peers += [(d, (t + j) % NT) for j in range(1, NT)]
    peers += [partner, sibling]
    for peer in peers:
        pl.semaphore_signal(barrier, inc=1, device_id=peer, device_id_type=MESH)
    pl.semaphore_wait(barrier, len(peers))

    def remote(src, dst, send, recv, peer):
        return pltpu.make_async_remote_copy(
            src_ref=src, dst_ref=dst, send_sem=send, recv_sem=recv,
            device_id=peer, device_id_type=MESH,
        )

    def place(p):
        slot, way = p // 2, p % 2
        hops = (slot + 1) // 2
        flag = jnp.where((slot == 0) | (slot == 7), way, (slot + 1) % 2)
        zs = (z + NZ + (2 * way - 1) * hops) % NZ
        return zs, (h + flag) % 2

    def z_copy(p, q, peer, send):
        zs, hs = place(p)
        ref = weights.at[zs, hs, c]
        return remote(ref, ref, send, brecv.at[q], peer)

    def sib_copy(p):
        zs, hs = place(p)
        ref = weights.at[zs, hs, c]
        return remote(ref, ref, ssend.at[p], srecv.at[p], sibling)

    def seed_copy():
        ref = weights.at[z, h, c]
        return remote(ref, ref, bsend2.at[2], brecv.at[1], partner)

    loads[0].wait()
    z_copy(0, 2, zup, bsend.at[0]).start()
    z_copy(0, 3, zdown, bsend2.at[0]).start()
    seed_copy().start()

    blk = tokens // NT
    eye = lax.broadcasted_iota(jnp.int32, (blk, blk), 0) == lax.broadcasted_iota(
        jnp.int32, (blk, blk), 1
    )
    for load in loads[1:]:
        load.wait()

    def rank_part(m, carry):
        rows = pl.ds(pl.multiple_of(m * 256, 256), 256)
        left = hid[rows, :]
        raw = lax.dot_general(left, ain[...], LAST, preferred_element_type=F32)
        wide = left.astype(F32)
        square = jnp.sum(wide * wide, axis=1, keepdims=True)
        later = lax.dot_general(cot[rows, :], aout[...], LAST, preferred_element_type=F32)
        for jj in range(256 // blk):
            j = m * (256 // blk) + jj
            cut = slice(jj * blk, (jj + 1) * blk)
            rsend[j, 0:blk, 0:256] = raw[cut]
            rsend[j, 0:blk, 256:512] = later[cut]
            rsend[j, blk : blk + 8, :] = jnp.zeros((8, 512), F32)
            rsend[j, blk : blk + 1, 0:blk] = jnp.sum(
                jnp.where(eye, square[cut], 0.0), axis=0, keepdims=True
            )
        return carry

    lax.fori_loop(0, tokens // 256, rank_part, 0)

    def rank_copy(j):
        to = (t + j) % NT
        return remote(
            rsend.at[to], rrecv.at[j - 1], rsend_sem.at[j - 1], rrecv_sem.at[j - 1], (d, to)
        )

    def td_copy(j):
        to = (t + j) % NT
        return remote(td.at[t], td.at[t], asend_sem.at[j - 1], arecv_sem.at[j - 1], (d, to))

    def td_arrival(j):
        ref = td.at[(t + NT - j) % NT]
        return remote(ref, ref, asend_sem.at[j - 1], arecv_sem.at[j - 1], (d, (t + j) % NT))

    for j in range(1, NT):
        rank_copy(j).start()

    def tangent_step():
        for j in range(1, NT):
            rank_copy(j).wait_recv()
        total = rsend[t]
        for j in range(1, NT):
            total = total + rrecv[j - 1]
        square_sum = jnp.sum(
            jnp.where(eye, total[blk : blk + 1, 0:blk], 0.0), axis=1, keepdims=True
        )
        lorentz_raw, later = total[:blk, 0:256], adapter_scale * total[:blk, 256:512]
        level = jnp.sqrt(square_sum / features + tiny_eps)
        lift = lift_of(exp_rate * level)
        lorentz = lift * lorentz_raw
        norm = jnp.sqrt(jnp.sum(lorentz * lorentz, axis=1, keepdims=True) + tiny_eps)
        root = jnp.sqrt(1.0 + norm * norm)
        phi = jnp.log(norm + root) / norm
        inner = jnp.sum(lorentz * later, axis=1, keepdims=True)
        coefficient = (1.0 / root - phi) / (norm * norm)
        dlorentz = phi * later + (coefficient * inner) * lorentz
        td[t, 0] = (phi * lorentz).astype(BF16)
        td[t, 1] = (lift * dlorentz).astype(BF16)
        for j in range(1, NT):
            td_copy(j).start()

    width = gpart.shape[-1]
    half = width // 2

    def g1_copy():
        return remote(gpart.at[1 - c], g1recv, g12send_sem.at[0], g12recv_sem.at[0], sibling)

    def g2_copy():
        return remote(g2send, g2recv, g12send_sem.at[1], g12recv_sem.at[1], partner)

    def g3_copy(i):
        to = (z + i) % NZ
        return remote(
            g3send.at[to], g3recv.at[i - 1], g3send_sem.at[i - 1], g3recv_sem.at[i - 1],
            at(to, h, c),
        )

    def grad_step():
        for j in range(1, NT):
            td_arrival(j).wait_recv()
        tangent = td[:, 0].reshape(tokens, 256)
        draw = td[:, 1].reshape(tokens, 256)

        def put(value, cols):
            for k in range(32):
                gpart[k % 2, (k // 2) % 2, k // 4, :, cols] = value[k * 8 : (k + 1) * 8]

        def in_tile(n, carry):
            cols = pl.ds(pl.multiple_of(n * 256, 256), 256)
            put(lax.dot_general(draw, hid[:, cols], FIRST, preferred_element_type=F32), cols)
            return carry

        lax.fori_loop(0, hid.shape[1] // 256, in_tile, 0)
        for n in range(2):
            cols = slice(n * 256, (n + 1) * 256)
            part = lax.dot_general(tangent, cot[:, cols], FIRST, preferred_element_type=F32)
            put(adapter_scale * part, slice(hid.shape[1] + n * 256, hid.shape[1] + (n + 1) * 256))
        g1_copy().start()
        for n in range(2):
            adapt[n] = adapter_scale * jnp.dot(
                tangent, aout[:, n * 256 : (n + 1) * 256], preferred_element_type=F32
            )

    def grad_two():
        g1_copy().wait_recv()
        g2send[...] = (gpart[c, 1 - h] + g1recv[1 - h]).reshape(64, width).astype(BF16)
        g2_copy().start()
        gpart[c, h] = gpart[c, h] + g1recv[h]

    def grad_three():
        g2_copy().wait_recv()
        gpart[c, h] = gpart[c, h] + g2recv[...].astype(F32).reshape(NZ, 8, width)
        for k in range(NZ):
            block = gpart[c, h, k]
            g3send[k] = jnp.concatenate([block[:, :half], block[:, half:]], axis=0).astype(BF16)
        for i in range(1, NZ):
            g3_copy(i).start()

    def grad_last():
        block = gpart[c, h, z]
        total = jnp.concatenate([block[:, :half], block[:, half:]], axis=0)
        for i in range(1, NZ):
            g3_copy(i).wait_recv()
            total = total + g3recv[i - 1].astype(F32)
        cut = hid.shape[1] - half
        gin_ref[:, :half] = total[:8]
        gin_ref[:, half:] = total[8:, :cut]
        gout_ref[...] = total[8:, cut:]

    def part_copy(p):
        zs, hs = place(p)
        to = zs % NY
        idx, src = (zs // NY) * 2 + hs, (y - to + NY - 1) % NY
        return remote(
            psend.at[p], precv.at[idx, src], csend_sem.at[p], crecv_sem.at[idx, src],
            (d, xl * NY + to),
        )

    def part_arrival(idx, src):
        ref = precv.at[idx, src]
        return remote(ref, ref, csend_sem.at[0], crecv_sem.at[idx, src], sibling)

    def x_copy(hs):
        return remote(
            xsend.at[hs], xrecv.at[hs], xsend_sem.at[hs], xrecv_sem.at[hs], (d, (1 - xl) * NY + y)
        )

    def reduce_strip(p):
        zs, hs = place(p)
        idx = (zs // NY) * 2 + hs

        @pl.when(zs % NY == y)
        def _():
            for src in range(NY - 1):
                part_arrival(idx, src).wait_recv()
            keep = zs // NY == xl

            def tile(m, carry):
                rows = pl.ds(pl.multiple_of(m * 128, 128), 128)
                value = acc[idx, rows, :]
                for src in range(NY - 1):
                    value = value + precv[idx, src, rows, :].astype(F32)
                acc[idx, rows, :] = value
                xsend[jnp.where(keep, 2, hs), rows, :] = value.astype(BF16)
                return carry

            lax.fori_loop(0, tokens // 128, tile, 0)

            @pl.when(jnp.logical_not(keep))
            def _():
                x_copy(hs).start()

    def step(p, carry):
        zs, hs = place(p)
        way = p % 2

        @pl.when(p >= 1)
        def _():
            z_copy(p, p, sibling, bsend.at[p]).wait_recv()

        @pl.when(p == 1)
        def _():
            z_copy(p, 4, zup, bsend.at[p]).start()
            z_copy(p, 5, zdown, bsend2.at[1]).start()

        @pl.when((p >= 2) & (p <= 10))
        def _():
            z_copy(p, p + 4, at((z + NZ + 1 - 2 * way) % NZ, h, c), bsend.at[p]).start()

        @pl.when(p == 13)
        def _():
            z_copy(p, 15, zdown, bsend.at[p]).start()

        sib_copy(p).start()
        sib_copy_in(p).wait_recv()
        to = zs % NY
        slot = jnp.where(to == y, (zs // NY) * 2 + hs, 4)

        def tile(m, inner):
            rows = pl.ds(pl.multiple_of(m * 256, 256), 256)
            right = jnp.concatenate([weights[zs, hs, 0], weights[zs, hs, 1]], axis=1)
            value = jnp.dot(hid[rows, :], right, preferred_element_type=F32)
            acc[slot, rows, :] = value
            psend[p, rows, :] = value.astype(BF16)
            return inner

        lax.fori_loop(0, tokens // 256, tile, 0)

        @pl.when(to != y)
        def _():
            part_copy(p).start()

        @pl.when(p >= LAG)
        def _():
            reduce_strip(p - LAG)

        @pl.when(p == 3)
        def _():
            tangent_step()

        @pl.when(p == 5)
        def _():
            grad_step()

        @pl.when(p == 7)
        def _():
            grad_two()

        @pl.when(p == 9)
        def _():
            grad_three()

        return carry

    def sib_copy_in(p):
        zs, hs = place(p)
        ref = weights.at[zs, hs, 1 - c]
        return remote(ref, ref, ssend.at[p], srecv.at[p], sibling)

    lax.fori_loop(0, 16, step, 0)

    def late(p, carry):
        reduce_strip(p)
        return carry

    lax.fori_loop(16 - LAG, 16, late, 0)
    grad_last()
    for n in range(2):
        x_copy(n).wait_recv()

        def last(m, carry, n=n):
            rows = pl.ds(pl.multiple_of(m * 128, 128), 128)
            value = acc[xl * 2 + n, rows, :] + xrecv[n, rows, :].astype(F32) + adapt[n, rows, :]
            out_ref[rows, n * 256 : (n + 1) * 256] = value.astype(BF16)
            return carry

        lax.fori_loop(0, tokens // 128, last, 0)

    z_copy(0, 2, zup, bsend.at[0]).wait_send()
    z_copy(0, 3, zdown, bsend2.at[0]).wait_send()
    seed_copy().wait_send()
    z_copy(1, 5, zdown, bsend2.at[1]).wait_send()

    def drain(p, carry):
        @pl.when(((p >= 1) & (p <= 10)) | (p == 13))
        def _():
            z_copy(p, p, zup, bsend.at[p]).wait_send()

        sib_copy(p).wait_send()
        zs, hs = place(p)

        @pl.when(zs % NY != y)
        def _():
            part_copy(p).wait_send()

        return carry

    lax.fori_loop(0, 16, drain, 0)
    for n in range(2):
        x_copy(n).wait_send()
    for j in range(1, NT):
        rank_copy(j).wait_send()
        td_copy(j).wait_send()
        g3_copy(j).wait_send()
    g1_copy().wait_send()
    g2_copy().wait_send()


def shards(hidden, base_weight, adapter_in, adapter_out, cotangent):
    tokens, ff = hidden.shape
    rank, cols = adapter_out.shape
    features = ff * lax.axis_size("tensor")
    width = ff + cols
    dma = pltpu.SemaphoreType.DMA
    hbm = pl.BlockSpec(memory_space=pl.ANY)
    vmem = pl.BlockSpec(memory_space=pltpu.VMEM)
    output, grad_in, grad_out = pl.pallas_call(
        functools.partial(kernel, features),
        out_shape=(
            jax.ShapeDtypeStruct((tokens, cols), BF16),
            jax.ShapeDtypeStruct((8, ff), F32),
            jax.ShapeDtypeStruct((8, cols), F32),
        ),
        in_specs=[hbm] * 5,
        out_specs=(vmem,) * 3,
        scratch_shapes=[
            pltpu.VMEM((tokens, ff), BF16),
            pltpu.VMEM((rank, ff), BF16),
            pltpu.VMEM((rank, cols), BF16),
            pltpu.VMEM((tokens, cols), BF16),
            pltpu.VMEM((NZ, 2, 2, ff, 128), BF16),
            pltpu.VMEM((16, tokens, 256), BF16),
            pltpu.VMEM((4, 3, tokens, 256), BF16),
            pltpu.VMEM((5, tokens, 256), F32),
            pltpu.VMEM((3, tokens, 256), BF16),
            pltpu.VMEM((2, tokens, 256), BF16),
            pltpu.VMEM((NT, tokens // NT + 8, 512), F32),
            pltpu.VMEM((NT - 1, tokens // NT + 8, 512), F32),
            pltpu.VMEM((NT, 2, tokens // NT, rank), BF16),
            pltpu.VMEM((2, 2, NZ, 8, width), F32),
            pltpu.VMEM((2, NZ, 8, width), F32),
            pltpu.VMEM((NZ * 8, width), BF16),
            pltpu.VMEM((NZ * 8, width), BF16),
            pltpu.VMEM((NZ, 16, width // 2), BF16),
            pltpu.VMEM((NZ - 1, 16, width // 2), BF16),
            pltpu.VMEM((2, tokens, 256), F32),
            dma((5,)),
            dma((16,)),
            dma((3,)),
            dma((16,)),
            dma((16,)),
            dma((16,)),
            dma((16,)),
            dma((4, 3)),
            dma((2,)),
            dma((2,)),
            dma((7,)),
            dma((7,)),
            dma((7,)),
            dma((7,)),
            dma((2,)),
            dma((2,)),
            dma((7,)),
            dma((7,)),
        ],
        compiler_params=pltpu.CompilerParams(
            collective_id=0, has_side_effects=True, vmem_limit_bytes=56 << 20
        ),
        name="adapter_step",
    )(hidden, base_weight, adapter_in, adapter_out, cotangent)
    return (output, grad_in, grad_out)


def solution(mesh):
    return jax.shard_map(
        shards,
        mesh=mesh,
        in_specs=(
            P("dp", "tensor"),
            P("tensor", "dp"),
            P(None, "tensor"),
            P(None, "tensor"),
            P("dp", "tensor"),
        ),
        out_specs=(P("dp", "tensor"), P("dp", "tensor"), P("dp", "tensor")),
        check_vma=False,
    )
```

```python
import functools

import jax
import jax.numpy as jnp
from jax import lax
from jax.experimental import pallas as pl
from jax.experimental.pallas import tpu as pltpu
from jax.sharding import PartitionSpec as P

adapter_scale = 4.0
exp_rate = 0.25
tiny_eps = 1e-06

MESH = pl.DeviceIdType.MESH
NZ, NY, NT = 8, 4, 8
F32, BF16 = jnp.float32, jnp.bfloat16
LAST = (((1,), (1,)), ((), ()))
FIRST = (((0,), (0,)), ((), ()))
LAG = 8
OFFSET = (0, 7, 1, 0, 6, 2, 7, 1, 5, 3, 6, 2, 4, 5, 3, 4)
OTHER = (0, 0, 0, 1, 0, 0, 1, 1, 0, 0, 1, 1, 0, 1, 1, 1)
SOURCE = (None, 0, 0, 0, 1, 2, 3, 3, 4, 5, 4, 5, None, 10, 11, 12)
UP, DOWN = (1, 4, 6, 8, 13), (2, 5, 7, 9, 14)


def lift_of(radius):
    sq = radius * radius
    series = 1.0 + sq / 6.0 * (
        1.0 + sq / 20.0 * (1.0 + sq / 42.0 * (1.0 + sq / 72.0 * (1.0 + sq / 110.0)))
    )
    direct = (jnp.exp(radius) - jnp.exp(-radius)) / (2.0 * radius)
    return jnp.where(radius < 1.0, series, direct)


def kernel(
    features,
    hid_hbm, b_hbm, ain_hbm, aout_hbm, cot_hbm,
    out_ref, gin_ref, gout_ref,
    hid, ain, aout, cot, weights, psend, precv, acc, xsend, xrecv,
    rsend, rrecv, td, gpart, g1recv, g2send, g2recv, g3send, g3recv, adapt,
    local_sem, bsend, brecv, ssend, srecv, csend_sem, crecv_sem,
    xsend_sem, xrecv_sem, rsend_sem, rrecv_sem, asend_sem, arecv_sem,
    g12send_sem, g12recv_sem, g3send_sem, g3recv_sem,
):
    d, t = lax.axis_index("dp"), lax.axis_index("tensor")
    z, h, c = d // 4, (d // 2) % 2, d % 2
    xl, y = t // NY, t % NY
    tokens = hid.shape[0]

    def at(z_, h_, c_):
        return (z_ * 4 + h_ * 2 + c_, t)

    zup, zdown = at((z + 1) % NZ, h, c), at((z + NZ - 1) % NZ, h, c)
    partner, sibling = at(z, 1 - h, c), at(z, h, 1 - c)

    loads = [
        pltpu.make_async_copy(b_hbm, weights.at[z, h, c], local_sem.at[0]),
        pltpu.make_async_copy(hid_hbm, hid, local_sem.at[1]),
        pltpu.make_async_copy(ain_hbm, ain, local_sem.at[2]),
        pltpu.make_async_copy(cot_hbm, cot, local_sem.at[3]),
        pltpu.make_async_copy(aout_hbm, aout, local_sem.at[4]),
    ]
    for load in loads:
        load.start()

    barrier = pltpu.get_barrier_semaphore()
    peers = [at((z + i) % NZ, h, c) for i in range(1, NZ)]
    peers += [(d, (t + j) % NT) for j in range(1, NT)]
    peers += [partner, sibling]
    for peer in peers:
        pl.semaphore_signal(barrier, inc=1, device_id=peer, device_id_type=MESH)
    pl.semaphore_wait(barrier, len(peers))

    def remote(src, dst, send, recv, peer):
        return pltpu.make_async_remote_copy(
            src_ref=src, dst_ref=dst, send_sem=send, recv_sem=recv,
            device_id=peer, device_id_type=MESH,
        )

    deep = hid.shape[1] // 48 * 16
    cuts = (pl.ds(0, deep), pl.ds(deep, hid.shape[1] - deep))

    def look(p, table):
        if isinstance(p, int):
            return table[p]
        return sum(jnp.where(p == i, v, 0) for i, v in enumerate(table) if v)

    def place(p):
        return (z + look(p, OFFSET)) % NZ, (h + look(p, OTHER)) % 2

    def piece(p, core, part):
        zs, hs = place(p)
        return weights.at[zs, hs, core, cuts[part]]

    def forward(q, part):
        if q == 12:
            up = (part + c) % 2 == 0
            ref = weights.at[(z + jnp.where(up, 5, 3)) % NZ, h, c, cuts[part]]
            peer = at((z + jnp.where(up, 1, NZ - 1)) % NZ, h, c)
        else:
            ref = piece(SOURCE[q], c, part)
            peer = zup if q in UP else zdown if q in DOWN else partner
        return remote(ref, ref, bsend.at[q, part], brecv.at[q, part], peer)

    def arrival(q, part):
        ref = piece(q, c, part)
        return remote(ref, ref, bsend.at[q, part], brecv.at[q, part], partner)

    def share(p, part, core):
        ref = piece(p, core, part)
        return remote(ref, ref, ssend.at[p, part], srecv.at[p, part], sibling)

    loads[0].wait()
    for part in range(2):
        for q in (1, 2, 3):
            forward(q, part).start()
    for part in range(2):
        share(0, part, c).start()

    groups = {
        1: [[(1, (4,)), (2, (5,))]] * 2,
        3: [[(3, ())]] * 2,
        4: [[(4, (6, 10)), (5, (7, 11))]] * 2,
        6: [[(6, (8,)), (7, (9,))]] * 2,
        8: [[(8, ()), (9, (12,))]] * 2,
        10: [[(10, ()), (11, ())]] * 2,
        12: [[(12, (13, 14, 15))]] * 2,
        13: [[(13, ()), (14, ())]] * 2,
        15: [[(15, ())]] * 2,
    }

    def arrive(first):
        for part in range(2):
            for q, onward in groups[first][part]:
                arrival(q, part).wait_recv()
                for n in onward:
                    forward(n, part).start()
                share(q, part, c).start()

    blk = tokens // NT
    eye = lax.broadcasted_iota(jnp.int32, (blk, blk), 0) == lax.broadcasted_iota(
        jnp.int32, (blk, blk), 1
    )
    for load in loads[1:]:
        load.wait()

    def rank_part(m, carry):
        rows = pl.ds(pl.multiple_of(m * 256, 256), 256)
        left = hid[rows, :]
        raw = lax.dot_general(left, ain[...], LAST, preferred_element_type=F32)
        wide = left.astype(F32)
        square = jnp.sum(wide * wide, axis=1, keepdims=True)
        later = lax.dot_general(cot[rows, :], aout[...], LAST, preferred_element_type=F32)
        for jj in range(256 // blk):
            j = m * (256 // blk) + jj
            cut = slice(jj * blk, (jj + 1) * blk)
            rsend[j, 0:blk, 0:256] = raw[cut]
            rsend[j, 0:blk, 256:512] = later[cut]
            rsend[j, blk : blk + 8, :] = jnp.zeros((8, 512), F32)
            rsend[j, blk : blk + 1, 0:blk] = jnp.sum(
                jnp.where(eye, square[cut], 0.0), axis=0, keepdims=True
            )
        return carry

    lax.fori_loop(0, tokens // 256, rank_part, 0)

    def rank_copy(j):
        to = (t + j) % NT
        return remote(
            rsend.at[to], rrecv.at[j - 1], rsend_sem.at[j - 1], rrecv_sem.at[j - 1], (d, to)
        )

    def td_copy(j):
        to = (t + j) % NT
        return remote(td.at[t], td.at[t], asend_sem.at[j - 1], arecv_sem.at[j - 1], (d, to))

    def td_arrival(j):
        ref = td.at[(t + NT - j) % NT]
        return remote(ref, ref, asend_sem.at[j - 1], arecv_sem.at[j - 1], (d, (t + j) % NT))

    for j in range(1, NT):
        rank_copy(j).start()

    def tangent_step():
        for j in range(1, NT):
            rank_copy(j).wait_recv()
        total = rsend[t]
        for j in range(1, NT):
            total = total + rrecv[j - 1]
        square_sum = jnp.sum(
            jnp.where(eye, total[blk : blk + 1, 0:blk], 0.0), axis=1, keepdims=True
        )
        lorentz_raw, later = total[:blk, 0:256], adapter_scale * total[:blk, 256:512]
        level = jnp.sqrt(square_sum / features + tiny_eps)
        lift = lift_of(exp_rate * level)
        lorentz = lift * lorentz_raw
        norm = jnp.sqrt(jnp.sum(lorentz * lorentz, axis=1, keepdims=True) + tiny_eps)
        root = jnp.sqrt(1.0 + norm * norm)
        phi = jnp.log(norm + root) / norm
        inner = jnp.sum(lorentz * later, axis=1, keepdims=True)
        coefficient = (1.0 / root - phi) / (norm * norm)
        dlorentz = phi * later + (coefficient * inner) * lorentz
        td[t, 0] = (phi * lorentz).astype(BF16)
        td[t, 1] = (lift * dlorentz).astype(BF16)
        for j in range(1, NT):
            td_copy(j).start()

    width = gpart.shape[-1]
    half = width // 2

    def g1_copy():
        return remote(gpart.at[1 - c], g1recv, g12send_sem.at[0], g12recv_sem.at[0], sibling)

    def g2_copy():
        return remote(g2send, g2recv, g12send_sem.at[1], g12recv_sem.at[1], partner)

    def g3_copy(i):
        to = (z + i) % NZ
        return remote(
            g3send.at[to], g3recv.at[i - 1], g3send_sem.at[i - 1], g3recv_sem.at[i - 1],
            at(to, h, c),
        )

    def grad_step():
        for j in range(1, NT):
            td_arrival(j).wait_recv()
        tangent = td[:, 0].reshape(tokens, 256)
        draw = td[:, 1].reshape(tokens, 256)

        def put(value, cols):
            for k in range(32):
                gpart[k % 2, (k // 2) % 2, k // 4, :, cols] = value[k * 8 : (k + 1) * 8]

        def in_tile(n, carry):
            cols = pl.ds(pl.multiple_of(n * 256, 256), 256)
            put(lax.dot_general(draw, hid[:, cols], FIRST, preferred_element_type=F32), cols)
            return carry

        lax.fori_loop(0, hid.shape[1] // 256, in_tile, 0)
        for n in range(2):
            cols = slice(n * 256, (n + 1) * 256)
            part = lax.dot_general(tangent, cot[:, cols], FIRST, preferred_element_type=F32)
            put(adapter_scale * part, slice(hid.shape[1] + n * 256, hid.shape[1] + (n + 1) * 256))
        g1_copy().start()
        for n in range(2):
            adapt[n] = adapter_scale * jnp.dot(
                tangent, aout[:, n * 256 : (n + 1) * 256], preferred_element_type=F32
            )

    def grad_two():
        g1_copy().wait_recv()
        g2send[...] = (gpart[c, 1 - h] + g1recv[1 - h]).reshape(64, width).astype(BF16)
        g2_copy().start()
        gpart[c, h] = gpart[c, h] + g1recv[h]

    def grad_three():
        g2_copy().wait_recv()
        gpart[c, h] = gpart[c, h] + g2recv[...].astype(F32).reshape(NZ, 8, width)
        for k in range(NZ):
            block = gpart[c, h, k]
            g3send[k] = jnp.concatenate([block[:, :half], block[:, half:]], axis=0).astype(BF16)
        for i in range(1, NZ):
            g3_copy(i).start()

    def grad_last():
        block = gpart[c, h, z]
        total = jnp.concatenate([block[:, :half], block[:, half:]], axis=0)
        for i in range(1, NZ):
            g3_copy(i).wait_recv()
            total = total + g3recv[i - 1].astype(F32)
        cut = hid.shape[1] - half
        gin_ref[:, :half] = total[:8]
        gin_ref[:, half:] = total[8:, :cut]
        gout_ref[...] = total[8:, cut:]

    tall = tokens // 2

    def part_copy(p, m):
        zs, hs = place(p)
        to = zs % NY
        idx, src = (zs // NY) * 2 + hs, (y - to + NY - 1) % NY
        rows = pl.ds(m * tall, tall)
        return remote(
            psend.at[p, rows], precv.at[idx, src, rows],
            csend_sem.at[p, m], crecv_sem.at[idx, src, m], (d, xl * NY + to),
        )

    def part_arrival(idx, src, m):
        ref = precv.at[idx, src, pl.ds(m * tall, tall)]
        return remote(ref, ref, csend_sem.at[0, m], crecv_sem.at[idx, src, m], sibling)

    def x_copy(hs, m):
        rows = pl.ds(m * tall, tall)
        return remote(
            xsend.at[hs, rows], xrecv.at[hs, rows], xsend_sem.at[hs, m], xrecv_sem.at[hs, m],
            (d, (1 - xl) * NY + y),
        )

    def reduce_strip(p):
        zs, hs = place(p)
        idx = (zs // NY) * 2 + hs

        @pl.when(zs % NY == y)
        def _():
            keep = zs // NY == xl

            def tile(m, carry):
                for src in range(NY - 1):
                    part_arrival(idx, src, m).wait_recv()
                rows = pl.ds(pl.multiple_of(m * tall, tall), tall)
                value = acc[idx, rows, :]
                for src in range(NY - 1):
                    value = value + precv[idx, src, rows, :].astype(F32)
                acc[idx, rows, :] = value
                xsend[jnp.where(keep, 2, hs), rows, :] = value.astype(BF16)

                @pl.when(jnp.logical_not(keep))
                def _():
                    x_copy(hs, m).start()

                return carry

            lax.fori_loop(0, 2, tile, 0)

    def step(p, carry):
        zs, hs = place(p)
        for first in groups:

            @pl.when(p == first)
            def _(first=first):
                arrive(first)

        for part in range(2):
            share(p, part, 1 - c).wait_recv()
        to = zs % NY
        slot = jnp.where(to == y, (zs // NY) * 2 + hs, 4)

        def tile(m, inner):
            rows = pl.ds(pl.multiple_of(m * tall, tall), tall)
            right = jnp.concatenate([weights[zs, hs, 0], weights[zs, hs, 1]], axis=1)
            value = jnp.dot(hid[rows, :], right, preferred_element_type=F32)
            acc[slot, rows, :] = value
            psend[p, rows, :] = value.astype(BF16)

            @pl.when(to != y)
            def _():
                part_copy(p, m).start()

            return inner

        lax.fori_loop(0, 2, tile, 0)

        @pl.when(p >= LAG)
        def _():
            reduce_strip(p - LAG)

        @pl.when(p == 3)
        def _():
            tangent_step()

        @pl.when(p == 5)
        def _():
            grad_step()

        @pl.when(p == 11)
        def _():
            grad_two()

        @pl.when(p == 15)
        def _():
            grad_three()

        return carry

    lax.fori_loop(0, 16, step, 0)

    def late(p, carry):
        reduce_strip(p)
        return carry

    lax.fori_loop(16 - LAG, 16, late, 0)

    def last(i, carry):
        n, m = i // 2, i % 2
        x_copy(n, m).wait_recv()
        rows = pl.ds(pl.multiple_of(m * tall, tall), tall)
        value = acc[xl * 2 + n, rows, :] + xrecv[n, rows, :].astype(F32) + adapt[n, rows, :]
        out_ref[rows, pl.ds(pl.multiple_of(n * 256, 256), 256)] = value.astype(BF16)
        return carry

    lax.fori_loop(0, 4, last, 0)
    grad_last()

    for q in range(1, 16):
        for part in range(2):
            forward(q, part).wait_send()

    def drain(p, carry):
        zs, hs = place(p)
        for part in range(2):
            share(p, part, c).wait_send()

        @pl.when(zs % NY != y)
        def _():
            for m in range(2):
                part_copy(p, m).wait_send()

        return carry

    lax.fori_loop(0, 16, drain, 0)
    for n in range(2):
        for m in range(2):
            x_copy(n, m).wait_send()
    for j in range(1, NT):
        rank_copy(j).wait_send()
        td_copy(j).wait_send()
        g3_copy(j).wait_send()
    g1_copy().wait_send()
    g2_copy().wait_send()


def place_results(*refs):
    for i in range(3):
        refs[i + 3][...] = refs[i][...]


def shards(hidden, base_weight, adapter_in, adapter_out, cotangent):
    tokens, ff = hidden.shape
    rank, cols = adapter_out.shape
    features = ff * lax.axis_size("tensor")
    width = ff + cols
    dma = pltpu.SemaphoreType.DMA
    hbm = pl.BlockSpec(memory_space=pl.ANY)
    vmem = pl.BlockSpec(memory_space=pltpu.VMEM)
    results = (
        jax.ShapeDtypeStruct((tokens, cols), BF16),
        jax.ShapeDtypeStruct((8, ff), F32),
        jax.ShapeDtypeStruct((8, cols), F32),
    )
    made = pl.pallas_call(
        functools.partial(kernel, features),
        out_shape=results,
        in_specs=[hbm] * 5,
        out_specs=(vmem,) * 3,
        scratch_shapes=[
            pltpu.VMEM((tokens, ff), BF16),
            pltpu.VMEM((rank, ff), BF16),
            pltpu.VMEM((rank, cols), BF16),
            pltpu.VMEM((tokens, cols), BF16),
            pltpu.VMEM((NZ, 2, 2, ff, 128), BF16),
            pltpu.VMEM((16, tokens, 256), BF16),
            pltpu.VMEM((4, 3, tokens, 256), BF16),
            pltpu.VMEM((5, tokens, 256), F32),
            pltpu.VMEM((3, tokens, 256), BF16),
            pltpu.VMEM((2, tokens, 256), BF16),
            pltpu.VMEM((NT, tokens // NT + 8, 512), F32),
            pltpu.VMEM((NT - 1, tokens // NT + 8, 512), F32),
            pltpu.VMEM((NT, 2, tokens // NT, rank), BF16),
            pltpu.VMEM((2, 2, NZ, 8, width), F32),
            pltpu.VMEM((2, NZ, 8, width), F32),
            pltpu.VMEM((NZ * 8, width), BF16),
            pltpu.VMEM((NZ * 8, width), BF16),
            pltpu.VMEM((NZ, 16, width // 2), BF16),
            pltpu.VMEM((NZ - 1, 16, width // 2), BF16),
            pltpu.VMEM((2, tokens, 256), F32),
            dma((5,)),
            dma((16, 2)),
            dma((16, 2)),
            dma((16, 2)),
            dma((16, 2)),
            dma((16, 2)),
            dma((4, 3, 2)),
            dma((2, 2)),
            dma((2, 2)),
            dma((7,)),
            dma((7,)),
            dma((7,)),
            dma((7,)),
            dma((2,)),
            dma((2,)),
            dma((7,)),
            dma((7,)),
        ],
        compiler_params=pltpu.CompilerParams(
            collective_id=0, has_side_effects=True, vmem_limit_bytes=56 << 20
        ),
        name="adapter_step",
    )(hidden, base_weight, adapter_in, adapter_out, cotangent)
    return pl.pallas_call(
        place_results,
        out_shape=results,
        in_specs=[vmem] * 3,
        out_specs=(vmem,) * 3,
        name="place_results",
    )(*made)


def solution(mesh):
    return jax.shard_map(
        shards,
        mesh=mesh,
        in_specs=(
            P("dp", "tensor"),
            P("tensor", "dp"),
            P(None, "tensor"),
            P(None, "tensor"),
            P("dp", "tensor"),
        ),
        out_specs=(P("dp", "tensor"), P("dp", "tensor"), P("dp", "tensor")),
        check_vma=False,
    )
```

```python
import functools

import jax
import jax.numpy as jnp
from jax import lax
from jax.experimental import pallas as pl
from jax.experimental.pallas import tpu as pltpu
from jax.sharding import PartitionSpec as P

adapter_scale = 4.0
exp_rate = 0.25
tiny_eps = 1e-06

MESH = pl.DeviceIdType.MESH
NZ, NY, NT = 8, 4, 8
F32, BF16 = jnp.float32, jnp.bfloat16
LAST = (((1,), (1,)), ((), ()))
REDUCED = (0, 0, 0, 0, 0, 0, 0, 2, 2, 4, 4, 6, 6, 6, 6, 8)
OFFSET = (0, 7, 1, 0, 6, 2, 5, 3, 7, 1, 6, 2, 4, 5, 3, 4)
OTHER = (0, 0, 0, 1, 0, 0, 0, 0, 1, 1, 1, 1, 0, 1, 1, 1)
SOURCE = (None, 0, 0, 0, 1, 2, 4, 5, 3, 3, 4, 5, None, 10, 11, 12)
UP, DOWN = (1, 4, 6, 8, 13), (2, 5, 7, 9, 14)


def lift_of(radius):
    sq = radius * radius
    series = 1.0 + sq / 6.0 * (
        1.0 + sq / 20.0 * (1.0 + sq / 42.0 * (1.0 + sq / 72.0 * (1.0 + sq / 110.0)))
    )
    direct = (jnp.exp(radius) - jnp.exp(-radius)) / (2.0 * radius)
    return jnp.where(radius < 1.0, series, direct)


def kernel(
    features,
    hid_hbm, b_hbm, ain_hbm, aout_hbm, cot_hbm,
    out_ref, gin_ref, gout_ref,
    hid, ain, aout, cot, weights, psend, precv, acc, xsend, xrecv,
    rsend, rrecv, rcross, td, turned, gpart, g1recv, g2send, g2recv, g3send, g3recv, adapt,
    local_sem, bsend, brecv, ssend, srecv, csend_sem, crecv_sem,
    xsend_sem, xrecv_sem, rsend_sem, rrecv_sem, asend_sem, arecv_sem,
    g12send_sem, g12recv_sem, g3send_sem, g3recv_sem,
):
    d, t = lax.axis_index("dp"), lax.axis_index("tensor")
    z, h, c = d // 4, (d // 2) % 2, d % 2
    xl, y = t // NY, t % NY
    tokens = hid.shape[0]

    def at(z_, h_, c_):
        return (z_ * 4 + h_ * 2 + c_, t)

    zup, zdown = at((z + 1) % NZ, h, c), at((z + NZ - 1) % NZ, h, c)
    partner, sibling = at(z, 1 - h, c), at(z, h, 1 - c)

    loads = [
        pltpu.make_async_copy(b_hbm, weights.at[z, h, c], local_sem.at[0]),
        pltpu.make_async_copy(hid_hbm, hid, local_sem.at[1]),
        pltpu.make_async_copy(ain_hbm, ain, local_sem.at[2]),
        pltpu.make_async_copy(cot_hbm, cot, local_sem.at[3]),
        pltpu.make_async_copy(aout_hbm, aout, local_sem.at[4]),
    ]
    for load in loads:
        load.start()

    barrier = pltpu.get_barrier_semaphore()
    peers = [at((z + i) % NZ, h, c) for i in range(1, NZ)]
    peers += [(d, (t + j) % NT) for j in range(1, NT)]
    peers += [partner, sibling]
    for peer in peers:
        pl.semaphore_signal(barrier, inc=1, device_id=peer, device_id_type=MESH)
    pl.semaphore_wait(barrier, len(peers))

    def remote(src, dst, send, recv, peer):
        return pltpu.make_async_remote_copy(
            src_ref=src, dst_ref=dst, send_sem=send, recv_sem=recv,
            device_id=peer, device_id_type=MESH,
        )

    deep = hid.shape[1] // 48 * 16
    cuts = (pl.ds(0, deep), pl.ds(deep, hid.shape[1] - deep))

    def look(p, table):
        if isinstance(p, int):
            return table[p]
        return sum(jnp.where(p == i, v, 0) for i, v in enumerate(table) if v)

    def place(p):
        return (z + look(p, OFFSET)) % NZ, (h + look(p, OTHER)) % 2

    def piece(p, core, part):
        zs, hs = place(p)
        return weights.at[zs, hs, core, cuts[part]]

    def forward(q, part):
        if q == 12:
            up = (part + c) % 2 == 0
            ref = weights.at[(z + jnp.where(up, 5, 3)) % NZ, h, c, cuts[part]]
            peer = at((z + jnp.where(up, 1, NZ - 1)) % NZ, h, c)
        else:
            ref = piece(SOURCE[q], c, part)
            peer = zup if q in UP else zdown if q in DOWN else partner
        return remote(ref, ref, bsend.at[q, part], brecv.at[q, part], peer)

    def arrival(q, part):
        ref = piece(q, c, part)
        return remote(ref, ref, bsend.at[q, part], brecv.at[q, part], partner)

    def share(p, part, core):
        ref = piece(p, core, part)
        return remote(ref, ref, ssend.at[p, part], srecv.at[p, part], sibling)

    loads[0].wait()
    for part in range(2):
        for q in (1, 2, 3):
            forward(q, part).start()
    for part in range(2):
        share(0, part, c).start()

    groups = {
        1: ((1, (4,)), (2, (5,))),
        3: ((3, ()),),
        4: ((4, (6, 10, 8)), (5, (7, 11, 9))),
        6: ((6, ()), (7, (12,))),
        8: ((8, ()), (9, ())),
        10: ((10, (13,)), (11, (14,))),
        12: ((12, (15,)),),
        13: ((13, ()), (14, ())),
        15: ((15, ()),),
    }

    def arrive(first):
        for part in range(2):
            for q, onward in groups[first]:
                arrival(q, part).wait_recv()
                for n in onward:
                    forward(n, part).start()
                share(q, part, c).start()

    blk = tokens // NT
    eye = lax.broadcasted_iota(jnp.int32, (blk, blk), 0) == lax.broadcasted_iota(
        jnp.int32, (blk, blk), 1
    )
    for load in loads[1:]:
        load.wait()

    def rank_part(m, carry):
        rows = pl.ds(pl.multiple_of(m * 256, 256), 256)
        left = hid[rows, :]
        raw = lax.dot_general(left, ain[...], LAST, preferred_element_type=F32)
        wide = left.astype(F32)
        square = jnp.sum(wide * wide, axis=1, keepdims=True)
        later = lax.dot_general(cot[rows, :], aout[...], LAST, preferred_element_type=F32)
        for jj in range(256 // blk):
            block = m * (256 // blk) + jj
            j = (block % NY, block // NY)
            cut = slice(jj * blk, (jj + 1) * blk)
            rsend[*j, 0:blk, 0:256] = raw[cut]
            rsend[*j, 0:blk, 256:512] = later[cut]
            rsend[*j, blk : blk + 8, :] = jnp.zeros((8, 512), F32)
            rsend[*j, blk : blk + 1, 0:blk] = jnp.sum(
                jnp.where(eye, square[cut], 0.0), axis=0, keepdims=True
            )
        return carry

    lax.fori_loop(0, tokens // 256, rank_part, 0)

    flip = (d, (1 - xl) * NY + y)

    def along(i):
        return (d, xl * NY + (y + i) % NY)

    def rank_copy(i):
        return remote(
            rsend.at[(y + i) % NY], rrecv.at[i - 1], rsend_sem.at[i - 1], rrecv_sem.at[i - 1], along(i)
        )

    def rank_cross():
        return remote(rsend.at[y, 1 - xl], rcross, rsend_sem.at[3], rrecv_sem.at[3], flip)

    def td_cross():
        return remote(td.at[t], td.at[t], asend_sem.at[6], arecv_sem.at[6], flip)

    def td_copy(i, side):
        ref = td.at[(xl + side) % 2 * NY + y]
        k = side * 3 + i - 1
        return remote(ref, ref, asend_sem.at[k], arecv_sem.at[k], along(i))

    def td_arrival(i, side):
        ref = td.at[(xl + side) % 2 * NY + (y + NY - i) % NY]
        k = side * 3 + i - 1
        return remote(ref, ref, asend_sem.at[k], arecv_sem.at[k], along(i))

    for i in range(1, NY):
        rank_copy(i).start()

    def rank_step():
        for i in range(1, NY):
            rank_copy(i).wait_recv()
        for side in range(2):
            total = rsend[y, side]
            for i in range(1, NY):
                total = total + rrecv[i - 1, side]
            rsend[y, side] = total
        rank_cross().start()

    def tangent_step():
        rank_cross().wait_recv()
        total = rsend[y, xl] + rcross[...]
        square_sum = jnp.sum(
            jnp.where(eye, total[blk : blk + 1, 0:blk], 0.0), axis=1, keepdims=True
        )
        lorentz_raw, later = total[:blk, 0:256], adapter_scale * total[:blk, 256:512]
        level = jnp.sqrt(square_sum / features + tiny_eps)
        lift = lift_of(exp_rate * level)
        lorentz = lift * lorentz_raw
        norm = jnp.sqrt(jnp.sum(lorentz * lorentz, axis=1, keepdims=True) + tiny_eps)
        root = jnp.sqrt(1.0 + norm * norm)
        phi = jnp.log(norm + root) / norm
        inner = jnp.sum(lorentz * later, axis=1, keepdims=True)
        coefficient = (1.0 / root - phi) / (norm * norm)
        dlorentz = phi * later + (coefficient * inner) * lorentz
        td[t, 0] = (phi * lorentz).astype(BF16)
        td[t, 1] = (lift * dlorentz).astype(BF16)
        td_cross().start()
        for i in range(1, NY):
            td_copy(i, 0).start()

    def tangent_pass():
        ref = td.at[(1 - xl) * NY + y]
        remote(ref, ref, asend_sem.at[6], arecv_sem.at[6], flip).wait_recv()
        for i in range(1, NY):
            td_copy(i, 1).start()

    width = gpart.shape[-1]
    half = width // 2

    def g1_copy():
        return remote(gpart.at[1 - c], g1recv, g12send_sem.at[0], g12recv_sem.at[0], sibling)

    def g2_copy():
        return remote(g2send, g2recv, g12send_sem.at[1], g12recv_sem.at[1], partner)

    def g3_copy(i):
        to = (z + i) % NZ
        return remote(
            g3send.at[to], g3recv.at[i - 1], g3send_sem.at[i - 1], g3recv_sem.at[i - 1],
            at(to, h, c),
        )

    def grad_step():
        for side in range(2):
            for i in range(1, NY):
                td_arrival(i, side).wait_recv()
        tangent = td[:, 0].reshape(tokens, 256)
        turned[0] = tangent.T
        turned[1] = td[:, 1].reshape(tokens, 256).T

        def put(value, cols):
            for k in range(32):
                gpart[k % 2, (k // 2) % 2, k // 4, :, cols] = value[k * 8 : (k + 1) * 8]

        def in_tile(n, carry):
            cols = pl.ds(pl.multiple_of(n * 256, 256), 256)
            put(jnp.dot(turned[1], hid[:, cols], preferred_element_type=F32), cols)
            return carry

        lax.fori_loop(0, hid.shape[1] // 256, in_tile, 0)
        for n in range(2):
            cols = slice(n * 256, (n + 1) * 256)
            part = jnp.dot(turned[0], cot[:, cols], preferred_element_type=F32)
            put(adapter_scale * part, slice(hid.shape[1] + n * 256, hid.shape[1] + (n + 1) * 256))
        g1_copy().start()
        for n in range(2):
            adapt[n] = adapter_scale * jnp.dot(
                tangent, aout[:, n * 256 : (n + 1) * 256], preferred_element_type=F32
            )

    def grad_two():
        g1_copy().wait_recv()
        g2send[...] = (gpart[c, 1 - h] + g1recv[1 - h]).reshape(64, width).astype(BF16)
        g2_copy().start()
        gpart[c, h] = gpart[c, h] + g1recv[h]

    def grad_three():
        g2_copy().wait_recv()
        gpart[c, h] = gpart[c, h] + g2recv[...].astype(F32).reshape(NZ, 8, width)
        for k in range(NZ):
            block = gpart[c, h, k]
            g3send[k] = jnp.concatenate([block[:, :half], block[:, half:]], axis=0).astype(BF16)
        for i in range(1, NZ):
            g3_copy(i).start()

    def grad_last():
        block = gpart[c, h, z]
        total = jnp.concatenate([block[:, :half], block[:, half:]], axis=0)
        for i in range(1, NZ):
            g3_copy(i).wait_recv()
            total = total + g3recv[i - 1].astype(F32)
        cut = hid.shape[1] - half
        gin_ref[:, :half] = total[:8]
        gin_ref[:, half:] = total[8:, :cut]
        gout_ref[...] = total[8:, cut:]

    tall = tokens // 2

    def part_copy(p, m):
        zs, hs = place(p)
        to = zs % NY
        idx, src = (zs // NY) * 2 + hs, (y - to + NY - 1) % NY
        rows = pl.ds(m * tall, tall)
        return remote(
            psend.at[p, rows], precv.at[idx, src, rows],
            csend_sem.at[p, m], crecv_sem.at[idx, src, m], (d, xl * NY + to),
        )

    def part_arrival(idx, src, m):
        ref = precv.at[idx, src, pl.ds(m * tall, tall)]
        return remote(ref, ref, csend_sem.at[0, m], crecv_sem.at[idx, src, m], sibling)

    def x_copy(hs, m):
        rows = pl.ds(m * tall, tall)
        return remote(
            xsend.at[hs, rows], xrecv.at[hs, rows], xsend_sem.at[hs, m], xrecv_sem.at[hs, m],
            (d, (1 - xl) * NY + y),
        )

    def reduce_strip(p):
        zs, hs = place(p)
        idx = (zs // NY) * 2 + hs

        @pl.when(zs % NY == y)
        def _():
            keep = zs // NY == xl

            def tile(m, carry):
                for src in range(NY - 1):
                    part_arrival(idx, src, m).wait_recv()
                rows = pl.ds(pl.multiple_of(m * tall, tall), tall)
                value = acc[idx, rows, :]
                for src in range(NY - 1):
                    value = value + precv[idx, src, rows, :].astype(F32)
                acc[idx, rows, :] = value
                xsend[jnp.where(keep, 2, hs), rows, :] = value.astype(BF16)

                @pl.when(jnp.logical_not(keep))
                def _():
                    x_copy(hs, m).start()

                return carry

            lax.fori_loop(0, 2, tile, 0)

    def late(p, carry):
        reduce_strip(p)
        return carry

    phases = (
        (3, rank_step),
        (5, tangent_step),
        (5, tangent_pass),
        (12, grad_step),
        (14, grad_two),
        (15, grad_three),
    )

    def step(p, carry):
        zs, hs = place(p)
        for first in groups:

            @pl.when(p == first)
            def _(first=first):
                arrive(first)

        for part in range(2):
            share(p, part, 1 - c).wait_recv()
        to = zs % NY
        slot = jnp.where(to == y, (zs // NY) * 2 + hs, 4)

        def tile(m, inner):
            rows = pl.ds(pl.multiple_of(m * tall, tall), tall)
            right = jnp.concatenate([weights[zs, hs, 0], weights[zs, hs, 1]], axis=1)
            value = jnp.dot(hid[rows, :], right, preferred_element_type=F32)
            acc[slot, rows, :] = value
            psend[p, rows, :] = value.astype(BF16)

            @pl.when(to != y)
            def _():
                part_copy(p, m).start()

            return inner

        lax.fori_loop(0, 2, tile, 0)

        lax.fori_loop(look(p - 1, REDUCED), look(p, REDUCED), late, 0)

        for when, phase in phases:

            @pl.when(p == when)
            def _(phase=phase):
                phase()

        return carry

    lax.fori_loop(0, 16, step, 0)

    lax.fori_loop(REDUCED[-1], 16, late, 0)

    def last(i, carry):
        n, m = i // 2, i % 2
        x_copy(n, m).wait_recv()
        rows = pl.ds(pl.multiple_of(m * tall, tall), tall)
        value = acc[xl * 2 + n, rows, :] + xrecv[n, rows, :].astype(F32) + adapt[n, rows, :]
        out_ref[rows, pl.ds(pl.multiple_of(n * 256, 256), 256)] = value.astype(BF16)
        return carry

    lax.fori_loop(0, 4, last, 0)
    grad_last()

    for q in range(1, 16):
        for part in range(2):
            forward(q, part).wait_send()

    def drain(p, carry):
        zs, hs = place(p)
        for part in range(2):
            share(p, part, c).wait_send()

        @pl.when(zs % NY != y)
        def _():
            for m in range(2):
                part_copy(p, m).wait_send()

        return carry

    lax.fori_loop(0, 16, drain, 0)
    for n in range(2):
        for m in range(2):
            x_copy(n, m).wait_send()
    for i in range(1, NY):
        rank_copy(i).wait_send()
        td_copy(i, 0).wait_send()
        td_copy(i, 1).wait_send()
    rank_cross().wait_send()
    td_cross().wait_send()
    for i in range(1, NZ):
        g3_copy(i).wait_send()
    g1_copy().wait_send()
    g2_copy().wait_send()


def place_results(*refs):
    for i in range(3):
        refs[i + 3][...] = refs[i][...]


def shards(hidden, base_weight, adapter_in, adapter_out, cotangent):
    tokens, ff = hidden.shape
    rank, cols = adapter_out.shape
    features = ff * lax.axis_size("tensor")
    width = ff + cols
    dma = pltpu.SemaphoreType.DMA
    hbm = pl.BlockSpec(memory_space=pl.ANY)
    vmem = pl.BlockSpec(memory_space=pltpu.VMEM)
    results = (
        jax.ShapeDtypeStruct((tokens, cols), BF16),
        jax.ShapeDtypeStruct((8, ff), F32),
        jax.ShapeDtypeStruct((8, cols), F32),
    )
    made = pl.pallas_call(
        functools.partial(kernel, features),
        out_shape=results,
        in_specs=[hbm] * 5,
        out_specs=(vmem,) * 3,
        scratch_shapes=[
            pltpu.VMEM((tokens, ff), BF16),
            pltpu.VMEM((rank, ff), BF16),
            pltpu.VMEM((rank, cols), BF16),
            pltpu.VMEM((tokens, cols), BF16),
            pltpu.VMEM((NZ, 2, 2, ff, 128), BF16),
            pltpu.VMEM((16, tokens, 256), BF16),
            pltpu.VMEM((4, 3, tokens, 256), BF16),
            pltpu.VMEM((5, tokens, 256), F32),
            pltpu.VMEM((3, tokens, 256), BF16),
            pltpu.VMEM((2, tokens, 256), BF16),
            pltpu.VMEM((NY, 2, tokens // NT + 8, 512), F32),
            pltpu.VMEM((NY - 1, 2, tokens // NT + 8, 512), F32),
            pltpu.VMEM((tokens // NT + 8, 512), F32),
            pltpu.VMEM((NT, 2, tokens // NT, rank), BF16),
            pltpu.VMEM((2, rank, tokens), BF16),
            pltpu.VMEM((2, 2, NZ, 8, width), F32),
            pltpu.VMEM((2, NZ, 8, width), F32),
            pltpu.VMEM((NZ * 8, width), BF16),
            pltpu.VMEM((NZ * 8, width), BF16),
            pltpu.VMEM((NZ, 16, width // 2), BF16),
            pltpu.VMEM((NZ - 1, 16, width // 2), BF16),
            pltpu.VMEM((2, tokens, 256), F32),
            dma((5,)),
            dma((16, 2)),
            dma((16, 2)),
            dma((16, 2)),
            dma((16, 2)),
            dma((16, 2)),
            dma((4, 3, 2)),
            dma((2, 2)),
            dma((2, 2)),
            dma((4,)),
            dma((4,)),
            dma((7,)),
            dma((7,)),
            dma((2,)),
            dma((2,)),
            dma((7,)),
            dma((7,)),
        ],
        compiler_params=pltpu.CompilerParams(
            collective_id=0, has_side_effects=True, vmem_limit_bytes=56 << 20
        ),
        name="adapter_step",
    )(hidden, base_weight, adapter_in, adapter_out, cotangent)
    return pl.pallas_call(
        place_results,
        out_shape=results,
        in_specs=[vmem] * 3,
        out_specs=(vmem,) * 3,
        name="place_results",
    )(*made)


def solution(mesh):
    return jax.shard_map(
        shards,
        mesh=mesh,
        in_specs=(
            P("dp", "tensor"),
            P("tensor", "dp"),
            P(None, "tensor"),
            P(None, "tensor"),
            P("dp", "tensor"),
        ),
        out_specs=(P("dp", "tensor"), P("dp", "tensor"), P("dp", "tensor")),
        check_vma=False,
    )
```

```python
import functools

import jax
import jax.numpy as jnp
from jax import lax
from jax.experimental import pallas as pl
from jax.experimental.pallas import tpu as pltpu
from jax.sharding import PartitionSpec as P

adapter_scale = 4.0
exp_rate = 0.25
tiny_eps = 1e-06

MESH = pl.DeviceIdType.MESH
NZ, NY, NT = 8, 4, 8
F32, BF16 = jnp.float32, jnp.bfloat16
LAST = (((1,), (1,)), ((), ()))
REDUCED = (0, 0, 0, 0, 0, 0, 0, 2, 2, 4, 4, 6, 6, 6, 6, 8)
OFFSET = (0, 7, 1, 0, 6, 2, 5, 3, 7, 1, 6, 2, 4, 5, 3, 4)
OTHER = (0, 0, 0, 1, 0, 0, 0, 0, 1, 1, 1, 1, 0, 1, 1, 1)
SOURCE = (None, 0, 0, 0, 1, 2, 4, 5, 3, 3, 4, 5, None, 10, 11, 12)
UP, DOWN = (1, 4, 6, 8, 13), (2, 5, 7, 9, 14)


def lift_of(radius):
    sq = radius * radius
    series = 1.0 + sq / 6.0 * (
        1.0 + sq / 20.0 * (1.0 + sq / 42.0 * (1.0 + sq / 72.0 * (1.0 + sq / 110.0)))
    )
    direct = (jnp.exp(radius) - jnp.exp(-radius)) / (2.0 * radius)
    return jnp.where(radius < 1.0, series, direct)


def kernel(
    features,
    hid_hbm, b_hbm, ain_hbm, aout_hbm, cot_hbm,
    out_ref, gin_ref, gout_ref,
    hid, ain, aout, cot, weights, psend, precv, acc, xsend, xrecv,
    rsend, rrecv, rcross, td, turned, gpart, g1recv, g2send, g2recv, g3send, g3recv, adapt,
    local_sem, bsend, brecv, ssend, srecv, csend_sem, crecv_sem,
    xsend_sem, xrecv_sem, rsend_sem, rrecv_sem, asend_sem, arecv_sem,
    g12send_sem, g12recv_sem, g3send_sem, g3recv_sem,
):
    d, t = lax.axis_index("dp"), lax.axis_index("tensor")
    z, h, c = d // 4, (d // 2) % 2, d % 2
    xl, y = t // NY, t % NY
    tokens = hid.shape[0]

    def at(z_, h_, c_):
        return (z_ * 4 + h_ * 2 + c_, t)

    zup, zdown = at((z + 1) % NZ, h, c), at((z + NZ - 1) % NZ, h, c)
    partner, sibling = at(z, 1 - h, c), at(z, h, 1 - c)

    loads = [
        pltpu.make_async_copy(b_hbm, weights.at[z, h, c], local_sem.at[0]),
        pltpu.make_async_copy(hid_hbm, hid, local_sem.at[1]),
        pltpu.make_async_copy(ain_hbm, ain, local_sem.at[2]),
        pltpu.make_async_copy(cot_hbm, cot, local_sem.at[3]),
        pltpu.make_async_copy(aout_hbm, aout, local_sem.at[4]),
    ]
    for load in loads:
        load.start()

    barrier = pltpu.get_barrier_semaphore()
    peers = [at((z + i) % NZ, h, c) for i in range(1, NZ)]
    peers += [(d, (t + j) % NT) for j in range(1, NT)]
    peers += [partner, sibling]
    for peer in peers:
        pl.semaphore_signal(barrier, inc=1, device_id=peer, device_id_type=MESH)
    pl.semaphore_wait(barrier, len(peers))

    def remote(src, dst, send, recv, peer):
        return pltpu.make_async_remote_copy(
            src_ref=src, dst_ref=dst, send_sem=send, recv_sem=recv,
            device_id=peer, device_id_type=MESH,
        )

    deep = hid.shape[1] // 48 * 16
    cuts = (pl.ds(0, deep), pl.ds(deep, hid.shape[1] - deep))

    def look(p, table):
        if isinstance(p, int):
            return table[p]
        return sum(jnp.where(p == i, v, 0) for i, v in enumerate(table) if v)

    def place(p):
        return (z + look(p, OFFSET)) % NZ, (h + look(p, OTHER)) % 2

    def piece(p, core, part):
        zs, hs = place(p)
        return weights.at[zs, hs, core, cuts[part]]

    def forward(q, part):
        if q == 12:
            up = (part + c) % 2 == 0
            ref = weights.at[(z + jnp.where(up, 5, 3)) % NZ, h, c, cuts[part]]
            peer = at((z + jnp.where(up, 1, NZ - 1)) % NZ, h, c)
        else:
            ref = piece(SOURCE[q], c, part)
            peer = zup if q in UP else zdown if q in DOWN else partner
        return remote(ref, ref, bsend.at[q, part], brecv.at[q, part], peer)

    def arrival(q, part):
        ref = piece(q, c, part)
        return remote(ref, ref, bsend.at[q, part], brecv.at[q, part], partner)

    def share(p, part, core):
        ref = piece(p, core, part)
        return remote(ref, ref, ssend.at[p, part], srecv.at[p, part], sibling)

    loads[0].wait()
    for part in range(2):
        for q in (1, 2, 3):
            forward(q, part).start()
    for part in range(2):
        share(0, part, c).start()

    groups = {
        1: [((1, (4,)), (2, (5,)))] * 2,
        3: [((3, ()),)] * 2,
        4: [((4, (6, 10)), (5, (7, 11))), ((4, (6, 10)), (5, (7, 11)))],
        6: [((6, (8,)), (7, (9, 12))), ((6, (8,)), (7, (9, 12)))],
        8: [((8, ()), (9, ()))] * 2,
        10: [((10, (13,)), (11, (14,)))] * 2,
        12: [((12, (15,)),)] * 2,
        13: [((13, ()), (14, ()))] * 2,
        15: [((15, ()),)] * 2,
    }

    def arrive(first):
        for part in range(2):
            for q, onward in groups[first][part]:
                arrival(q, part).wait_recv()
                for n in onward:
                    forward(n, part).start()
                share(q, part, c).start()

    blk = tokens // NT
    eye = lax.broadcasted_iota(jnp.int32, (blk, blk), 0) == lax.broadcasted_iota(
        jnp.int32, (blk, blk), 1
    )
    for load in loads[1:]:
        load.wait()

    def rank_part(m, carry):
        rows = pl.ds(pl.multiple_of(m * 256, 256), 256)
        left = hid[rows, :]
        raw = lax.dot_general(left, ain[...], LAST, preferred_element_type=F32)
        wide = left.astype(F32)
        square = jnp.sum(wide * wide, axis=1, keepdims=True)
        later = lax.dot_general(cot[rows, :], aout[...], LAST, preferred_element_type=F32)
        for jj in range(256 // blk):
            block = m * (256 // blk) + jj
            j = (block % NY, block // NY)
            cut = slice(jj * blk, (jj + 1) * blk)
            rsend[*j, 0:blk, 0:256] = raw[cut]
            rsend[*j, 0:blk, 256:512] = later[cut]
            rsend[*j, blk : blk + 8, :] = jnp.zeros((8, 512), F32)
            rsend[*j, blk : blk + 1, 0:blk] = jnp.sum(
                jnp.where(eye, square[cut], 0.0), axis=0, keepdims=True
            )
        return carry

    lax.fori_loop(0, tokens // 256, rank_part, 0)

    flip = (d, (1 - xl) * NY + y)

    def along(i):
        return (d, xl * NY + (y + i) % NY)

    def rank_copy(i):
        return remote(
            rsend.at[(y + i) % NY], rrecv.at[i - 1], rsend_sem.at[i - 1], rrecv_sem.at[i - 1], along(i)
        )

    def rank_cross():
        return remote(rsend.at[y, 1 - xl], rcross, rsend_sem.at[3], rrecv_sem.at[3], flip)

    def td_cross():
        return remote(td.at[t], td.at[t], asend_sem.at[6], arecv_sem.at[6], flip)

    def td_copy(i, side):
        ref = td.at[(xl + side) % 2 * NY + y]
        k = side * 3 + i - 1
        return remote(ref, ref, asend_sem.at[k], arecv_sem.at[k], along(i))

    def td_arrival(i, side):
        ref = td.at[(xl + side) % 2 * NY + (y + NY - i) % NY]
        k = side * 3 + i - 1
        return remote(ref, ref, asend_sem.at[k], arecv_sem.at[k], along(i))

    for i in range(1, NY):
        rank_copy(i).start()

    def rank_step():
        for i in range(1, NY):
            rank_copy(i).wait_recv()
        for side in range(2):
            total = rsend[y, side]
            for i in range(1, NY):
                total = total + rrecv[i - 1, side]
            rsend[y, side] = total
        rank_cross().start()

    def tangent_step():
        rank_cross().wait_recv()
        total = rsend[y, xl] + rcross[...]
        square_sum = jnp.sum(
            jnp.where(eye, total[blk : blk + 1, 0:blk], 0.0), axis=1, keepdims=True
        )
        lorentz_raw, later = total[:blk, 0:256], adapter_scale * total[:blk, 256:512]
        level = jnp.sqrt(square_sum / features + tiny_eps)
        lift = lift_of(exp_rate * level)
        lorentz = lift * lorentz_raw
        norm = jnp.sqrt(jnp.sum(lorentz * lorentz, axis=1, keepdims=True) + tiny_eps)
        root = jnp.sqrt(1.0 + norm * norm)
        phi = jnp.log(norm + root) / norm
        inner = jnp.sum(lorentz * later, axis=1, keepdims=True)
        coefficient = (1.0 / root - phi) / (norm * norm)
        dlorentz = phi * later + (coefficient * inner) * lorentz
        td[t, 0] = (phi * lorentz).astype(BF16)
        td[t, 1] = (lift * dlorentz).astype(BF16)
        td_cross().start()
        for i in range(1, NY):
            td_copy(i, 0).start()

    def tangent_pass():
        ref = td.at[(1 - xl) * NY + y]
        remote(ref, ref, asend_sem.at[6], arecv_sem.at[6], flip).wait_recv()
        for i in range(1, NY):
            td_copy(i, 1).start()

    width = gpart.shape[-1]
    half = width // 2

    def g1_copy():
        return remote(gpart.at[1 - c], g1recv, g12send_sem.at[0], g12recv_sem.at[0], sibling)

    def g2_copy():
        return remote(g2send, g2recv, g12send_sem.at[1], g12recv_sem.at[1], partner)

    def g3_copy(i):
        to = (z + i) % NZ
        return remote(
            g3send.at[to], g3recv.at[i - 1], g3send_sem.at[i - 1], g3recv_sem.at[i - 1],
            at(to, h, c),
        )

    def grad_step():
        for side in range(2):
            for i in range(1, NY):
                td_arrival(i, side).wait_recv()
        tangent = td[:, 0].reshape(tokens, 256)
        turned[0] = tangent.T
        turned[1] = td[:, 1].reshape(tokens, 256).T

        def put(value, cols):
            for k in range(32):
                gpart[k % 2, (k // 2) % 2, k // 4, :, cols] = value[k * 8 : (k + 1) * 8]

        def in_tile(n, carry):
            cols = pl.ds(pl.multiple_of(n * 256, 256), 256)
            put(jnp.dot(turned[1], hid[:, cols], preferred_element_type=F32), cols)
            return carry

        lax.fori_loop(0, hid.shape[1] // 256, in_tile, 0)
        for n in range(2):
            cols = slice(n * 256, (n + 1) * 256)
            part = jnp.dot(turned[0], cot[:, cols], preferred_element_type=F32)
            put(adapter_scale * part, slice(hid.shape[1] + n * 256, hid.shape[1] + (n + 1) * 256))
        g1_copy().start()
        for n in range(2):
            adapt[n] = adapter_scale * jnp.dot(
                tangent, aout[:, n * 256 : (n + 1) * 256], preferred_element_type=F32
            )

    def grad_two():
        g1_copy().wait_recv()
        g2send[...] = (gpart[c, 1 - h] + g1recv[1 - h]).reshape(64, width).astype(BF16)
        g2_copy().start()
        gpart[c, h] = gpart[c, h] + g1recv[h]

    def grad_three():
        g2_copy().wait_recv()
        gpart[c, h] = gpart[c, h] + g2recv[...].astype(F32).reshape(NZ, 8, width)
        for k in range(NZ):
            block = gpart[c, h, k]
            g3send[k] = jnp.concatenate([block[:, :half], block[:, half:]], axis=0).astype(BF16)
        for i in range(1, NZ):
            g3_copy(i).start()

    def grad_last():
        block = gpart[c, h, z]
        total = jnp.concatenate([block[:, :half], block[:, half:]], axis=0)
        for i in range(1, NZ):
            g3_copy(i).wait_recv()
            total = total + g3recv[i - 1].astype(F32)
        cut = hid.shape[1] - half
        gin_ref[:, :half] = total[:8]
        gin_ref[:, half:] = total[8:, :cut]
        gout_ref[...] = total[8:, cut:]

    tall = tokens // 2

    def part_copy(p, m):
        zs, hs = place(p)
        to = zs % NY
        idx, src = (zs // NY) * 2 + hs, (y - to + NY - 1) % NY
        rows = pl.ds(m * tall, tall)
        return remote(
            psend.at[p, rows], precv.at[idx, src, rows],
            csend_sem.at[p, m], crecv_sem.at[idx, src, m], (d, xl * NY + to),
        )

    def part_arrival(idx, src, m):
        ref = precv.at[idx, src, pl.ds(m * tall, tall)]
        return remote(ref, ref, csend_sem.at[0, m], crecv_sem.at[idx, src, m], sibling)

    def x_copy(hs, m):
        rows = pl.ds(m * tall, tall)
        return remote(
            xsend.at[hs, rows], xrecv.at[hs, rows], xsend_sem.at[hs, m], xrecv_sem.at[hs, m],
            (d, (1 - xl) * NY + y),
        )

    def reduce_strip(p):
        zs, hs = place(p)
        idx = (zs // NY) * 2 + hs

        @pl.when(zs % NY == y)
        def _():
            keep = zs // NY == xl

            def tile(m, carry):
                for src in range(NY - 1):
                    part_arrival(idx, src, m).wait_recv()
                rows = pl.ds(pl.multiple_of(m * tall, tall), tall)
                value = acc[idx, rows, :]
                for src in range(NY - 1):
                    value = value + precv[idx, src, rows, :].astype(F32)
                acc[idx, rows, :] = value
                xsend[jnp.where(keep, 2, hs), rows, :] = value.astype(BF16)

                @pl.when(jnp.logical_not(keep))
                def _():
                    x_copy(hs, m).start()

                return carry

            lax.fori_loop(0, 2, tile, 0)

    def late(p, carry):
        reduce_strip(p)
        return carry

    phases = ((3, rank_step), (5, tangent_step), (7, tangent_pass)) + (
        (12, grad_step), (14, grad_two), (15, grad_three),
    )

    def step(p, carry):
        zs, hs = place(p)
        for first in groups:

            @pl.when(p == first)
            def _(first=first):
                arrive(first)

        for part in range(2):
            share(p, part, 1 - c).wait_recv()
        to = zs % NY
        slot = jnp.where(to == y, (zs // NY) * 2 + hs, 4)

        def tile(m, inner):
            rows = pl.ds(pl.multiple_of(m * tall, tall), tall)
            right = jnp.concatenate([weights[zs, hs, 0], weights[zs, hs, 1]], axis=1)
            value = jnp.dot(hid[rows, :], right, preferred_element_type=F32)
            acc[slot, rows, :] = value
            psend[p, rows, :] = value.astype(BF16)

            @pl.when(to != y)
            def _():
                part_copy(p, m).start()

            return inner

        lax.fori_loop(0, 2, tile, 0)

        lax.fori_loop(look(p - 1, REDUCED), look(p, REDUCED), late, 0)

        for when, phase in phases:

            @pl.when(p == when)
            def _(phase=phase):
                phase()

        return carry

    lax.fori_loop(0, 16, step, 0)

    lax.fori_loop(REDUCED[-1], 16, late, 0)

    def last(i, carry):
        n, m = i // 2, i % 2
        x_copy(n, m).wait_recv()
        rows = pl.ds(pl.multiple_of(m * tall, tall), tall)
        value = acc[xl * 2 + n, rows, :] + xrecv[n, rows, :].astype(F32) + adapt[n, rows, :]
        out_ref[rows, pl.ds(pl.multiple_of(n * 256, 256), 256)] = value.astype(BF16)
        return carry

    lax.fori_loop(0, 4, last, 0)
    grad_last()

    for q in range(1, 16):
        for part in range(2):
            forward(q, part).wait_send()

    def drain(p, carry):
        zs, hs = place(p)
        for part in range(2):
            share(p, part, c).wait_send()

        @pl.when(zs % NY != y)
        def _():
            for m in range(2):
                part_copy(p, m).wait_send()

        return carry

    lax.fori_loop(0, 16, drain, 0)
    for n in range(2):
        for m in range(2):
            x_copy(n, m).wait_send()
    for i in range(1, NY):
        rank_copy(i).wait_send()
        td_copy(i, 0).wait_send()
        td_copy(i, 1).wait_send()
    rank_cross().wait_send()
    td_cross().wait_send()
    for i in range(1, NZ):
        g3_copy(i).wait_send()
    g1_copy().wait_send()
    g2_copy().wait_send()


def place_results(*refs):
    for i in range(3):
        refs[i + 3][...] = refs[i][...]


def shards(hidden, base_weight, adapter_in, adapter_out, cotangent):
    tokens, ff = hidden.shape
    rank, cols = adapter_out.shape
    features = ff * lax.axis_size("tensor")
    width = ff + cols
    dma = pltpu.SemaphoreType.DMA
    hbm = pl.BlockSpec(memory_space=pl.ANY)
    vmem = pl.BlockSpec(memory_space=pltpu.VMEM)
    results = (
        jax.ShapeDtypeStruct((tokens, cols), BF16),
        jax.ShapeDtypeStruct((8, ff), F32),
        jax.ShapeDtypeStruct((8, cols), F32),
    )
    made = pl.pallas_call(
        functools.partial(kernel, features),
        out_shape=results,
        in_specs=[hbm] * 5,
        out_specs=(vmem,) * 3,
        scratch_shapes=[
            pltpu.VMEM((tokens, ff), BF16),
            pltpu.VMEM((rank, ff), BF16),
            pltpu.VMEM((rank, cols), BF16),
            pltpu.VMEM((tokens, cols), BF16),
            pltpu.VMEM((NZ, 2, 2, ff, 128), BF16),
            pltpu.VMEM((16, tokens, 256), BF16),
            pltpu.VMEM((4, 3, tokens, 256), BF16),
            pltpu.VMEM((5, tokens, 256), F32),
            pltpu.VMEM((3, tokens, 256), BF16),
            pltpu.VMEM((2, tokens, 256), BF16),
            pltpu.VMEM((NY, 2, tokens // NT + 8, 512), F32),
            pltpu.VMEM((NY - 1, 2, tokens // NT + 8, 512), F32),
            pltpu.VMEM((tokens // NT + 8, 512), F32),
            pltpu.VMEM((NT, 2, tokens // NT, rank), BF16),
            pltpu.VMEM((2, rank, tokens), BF16),
            pltpu.VMEM((2, 2, NZ, 8, width), F32),
            pltpu.VMEM((2, NZ, 8, width), F32),
            pltpu.VMEM((NZ * 8, width), BF16),
            pltpu.VMEM((NZ * 8, width), BF16),
            pltpu.VMEM((NZ, 16, width // 2), BF16),
            pltpu.VMEM((NZ - 1, 16, width // 2), BF16),
            pltpu.VMEM((2, tokens, 256), F32),
            dma((5,)),
            dma((16, 2)),
            dma((16, 2)),
            dma((16, 2)),
            dma((16, 2)),
            dma((16, 2)),
            dma((4, 3, 2)),
            dma((2, 2)),
            dma((2, 2)),
            dma((4,)),
            dma((4,)),
            dma((7,)),
            dma((7,)),
            dma((2,)),
            dma((2,)),
            dma((7,)),
            dma((7,)),
        ],
        compiler_params=pltpu.CompilerParams(
            collective_id=0, has_side_effects=True, vmem_limit_bytes=56 << 20
        ),
        name="adapter_step",
    )(hidden, base_weight, adapter_in, adapter_out, cotangent)
    return pl.pallas_call(
        place_results,
        out_shape=results,
        in_specs=[vmem] * 3,
        out_specs=(vmem,) * 3,
        name="place_results",
    )(*made)


def solution(mesh):
    return jax.shard_map(
        shards,
        mesh=mesh,
        in_specs=(
            P("dp", "tensor"),
            P("tensor", "dp"),
            P(None, "tensor"),
            P(None, "tensor"),
            P("dp", "tensor"),
        ),
        out_specs=(P("dp", "tensor"), P("dp", "tensor"), P("dp", "tensor")),
        check_vma=False,
    )
```

```python
import functools

import jax
import jax.numpy as jnp
from jax import lax
from jax.experimental import pallas as pl
from jax.experimental.pallas import tpu as pltpu
from jax.sharding import PartitionSpec as P

adapter_scale = 4.0
exp_rate = 0.25
tiny_eps = 1e-06

MESH = pl.DeviceIdType.MESH
NZ, NY, NT = 8, 4, 8
F32, BF16 = jnp.float32, jnp.bfloat16
LAST = (((1,), (1,)), ((), ()))
REDUCED = (0, 0, 0, 0, 0, 0, 0, 2, 2, 4, 4, 6, 6, 6, 6, 8)
OFFSET = (0, 7, 1, 0, 6, 2, 5, 3, 7, 1, 6, 2, 4, 5, 3, 4)
OTHER = (0, 0, 0, 1, 0, 0, 0, 0, 1, 1, 1, 1, 0, 1, 1, 1)
SOURCE = (None, 0, 0, 0, 1, 2, 4, 5, 3, 3, 4, 5, None, 10, 11, 12)
UP, DOWN = (1, 4, 6, 8, 13), (2, 5, 7, 9, 14)


def lift_of(radius):
    sq = radius * radius
    series = 1.0 + sq / 6.0 * (
        1.0 + sq / 20.0 * (1.0 + sq / 42.0 * (1.0 + sq / 72.0 * (1.0 + sq / 110.0)))
    )
    direct = (jnp.exp(radius) - jnp.exp(-radius)) / (2.0 * radius)
    return jnp.where(radius < 1.0, series, direct)


def kernel(
    features,
    hid_hbm, b_hbm, ain_hbm, aout_hbm, cot_hbm,
    out_ref, gin_ref, gout_ref,
    hid, ain, aout, cot, weights, psend, precv, acc, xsend, xrecv,
    rsend, rrecv, rcross, td, turned, gpart, g1recv, g2send, g2recv, g3send, g3recv, adapt,
    local_sem, bsend, brecv, ssend, srecv, csend_sem, crecv_sem,
    xsend_sem, xrecv_sem, rsend_sem, rrecv_sem, asend_sem, arecv_sem,
    g12send_sem, g12recv_sem, g3send_sem, g3recv_sem,
):
    d, t = lax.axis_index("dp"), lax.axis_index("tensor")
    z, h, c = d // 4, (d // 2) % 2, d % 2
    xl, y = t // NY, t % NY
    tokens = hid.shape[0]

    def at(z_, h_, c_):
        return (z_ * 4 + h_ * 2 + c_, t)

    zup, zdown = at((z + 1) % NZ, h, c), at((z + NZ - 1) % NZ, h, c)
    partner, sibling = at(z, 1 - h, c), at(z, h, 1 - c)

    loads = [
        pltpu.make_async_copy(b_hbm, weights.at[z, h, c], local_sem.at[0]),
        pltpu.make_async_copy(hid_hbm, hid, local_sem.at[1]),
        pltpu.make_async_copy(ain_hbm, ain, local_sem.at[2]),
        pltpu.make_async_copy(cot_hbm, cot, local_sem.at[3]),
        pltpu.make_async_copy(aout_hbm, aout, local_sem.at[4]),
    ]
    for load in loads:
        load.start()

    barrier = pltpu.get_barrier_semaphore()
    peers = [at((z + i) % NZ, h, c) for i in range(1, NZ)]
    peers += [(d, (t + j) % NT) for j in range(1, NT)]
    peers += [partner, sibling]
    for peer in peers:
        pl.semaphore_signal(barrier, inc=1, device_id=peer, device_id_type=MESH)
    pl.semaphore_wait(barrier, len(peers))

    def remote(src, dst, send, recv, peer):
        return pltpu.make_async_remote_copy(
            src_ref=src, dst_ref=dst, send_sem=send, recv_sem=recv,
            device_id=peer, device_id_type=MESH,
        )

    deep = hid.shape[1] // 48 * 16
    cuts = (pl.ds(0, deep), pl.ds(deep, hid.shape[1] - deep))

    def look(p, table):
        if isinstance(p, int):
            return table[p]
        return sum(jnp.where(p == i, v, 0) for i, v in enumerate(table) if v)

    def place(p):
        return (z + look(p, OFFSET)) % NZ, (h + look(p, OTHER)) % 2

    def piece(p, core, part):
        zs, hs = place(p)
        return weights.at[zs, hs, core, cuts[part]]

    def forward(q, part):
        if q == 12:
            up = (part + c) % 2 == 0
            ref = weights.at[(z + jnp.where(up, 5, 3)) % NZ, h, c, cuts[part]]
            peer = at((z + jnp.where(up, 1, NZ - 1)) % NZ, h, c)
        else:
            ref = piece(SOURCE[q], c, part)
            peer = zup if q in UP else zdown if q in DOWN else partner
        return remote(ref, ref, bsend.at[q, part], brecv.at[q, part], peer)

    def arrival(q, part):
        ref = piece(q, c, part)
        return remote(ref, ref, bsend.at[q, part], brecv.at[q, part], partner)

    def share(p, part, core):
        ref = piece(p, core, part)
        return remote(ref, ref, ssend.at[p, part], srecv.at[p, part], sibling)

    loads[0].wait()
    for part in range(2):
        for q in (1, 2, 3):
            forward(q, part).start()
    for part in range(2):
        share(0, part, c).start()

    groups = {
        1: [((1, (4,)), (2, (5,)))] * 2,
        3: [((3, ()),)] * 2,
        4: [((4, (6, 10)), (5, (7, 11))), ((4, (6, 10)), (5, (7, 11)))],
        6: [((6, (8,)), (7, (9, 12))), ((6, (8,)), (7, (9, 12)))],
        8: [((8, ()), (9, ()))] * 2,
        10: [((10, (13,)), (11, (14,)))] * 2,
        12: [((12, (15,)),)] * 2,
        13: [((13, ()), (14, ()))] * 2,
        15: [((15, ()),)] * 2,
    }

    def arrive(first):
        for part in range(2):
            for q, onward in groups[first][part]:
                arrival(q, part).wait_recv()
                for n in onward:
                    forward(n, part).start()
                share(q, part, c).start()

    blk = tokens // NT
    eye = lax.broadcasted_iota(jnp.int32, (blk, blk), 0) == lax.broadcasted_iota(
        jnp.int32, (blk, blk), 1
    )
    for load in loads[1:]:
        load.wait()

    def rank_part(m, carry):
        rows = pl.ds(pl.multiple_of(m * 256, 256), 256)
        left = hid[rows, :]
        raw = lax.dot_general(left, ain[...], LAST, preferred_element_type=F32)
        wide = left.astype(F32)
        square = jnp.sum(wide * wide, axis=1, keepdims=True)
        later = lax.dot_general(cot[rows, :], aout[...], LAST, preferred_element_type=F32)
        for jj in range(256 // blk):
            block = m * (256 // blk) + jj
            j = (block % NY, block // NY)
            cut = slice(jj * blk, (jj + 1) * blk)
            rsend[*j, 0:blk, 0:256] = raw[cut]
            rsend[*j, 0:blk, 256:512] = later[cut]
            rsend[*j, blk : blk + 8, :] = jnp.zeros((8, 512), F32)
            rsend[*j, blk : blk + 1, 0:blk] = jnp.sum(
                jnp.where(eye, square[cut], 0.0), axis=0, keepdims=True
            )
        return carry

    lax.fori_loop(0, tokens // 256, rank_part, 0)

    flip = (d, (1 - xl) * NY + y)

    def along(i):
        return (d, xl * NY + (y + i) % NY)

    def rank_copy(i):
        return remote(
            rsend.at[(y + i) % NY], rrecv.at[i - 1], rsend_sem.at[i - 1], rrecv_sem.at[i - 1], along(i)
        )

    def rank_cross():
        return remote(rsend.at[y, 1 - xl], rcross, rsend_sem.at[3], rrecv_sem.at[3], flip)

    def td_cross():
        return remote(td.at[t], td.at[t], asend_sem.at[6], arecv_sem.at[6], flip)

    def td_copy(i, side):
        ref = td.at[(xl + side) % 2 * NY + y]
        k = side * 3 + i - 1
        return remote(ref, ref, asend_sem.at[k], arecv_sem.at[k], along(i))

    def td_arrival(i, side):
        ref = td.at[(xl + side) % 2 * NY + (y + NY - i) % NY]
        k = side * 3 + i - 1
        return remote(ref, ref, asend_sem.at[k], arecv_sem.at[k], along(i))

    for i in range(1, NY):
        rank_copy(i).start()

    def rank_step():
        for i in range(1, NY):
            rank_copy(i).wait_recv()
        for side in range(2):
            total = rsend[y, side]
            for i in range(1, NY):
                total = total + rrecv[i - 1, side]
            rsend[y, side] = total
        rank_cross().start()

    def tangent_step():
        rank_cross().wait_recv()
        total = rsend[y, xl] + rcross[...]
        square_sum = jnp.sum(
            jnp.where(eye, total[blk : blk + 1, 0:blk], 0.0), axis=1, keepdims=True
        )
        lorentz_raw, later = total[:blk, 0:256], adapter_scale * total[:blk, 256:512]
        level = jnp.sqrt(square_sum / features + tiny_eps)
        lift = lift_of(exp_rate * level)
        lorentz = lift * lorentz_raw
        norm = jnp.sqrt(jnp.sum(lorentz * lorentz, axis=1, keepdims=True) + tiny_eps)
        root = jnp.sqrt(1.0 + norm * norm)
        phi = jnp.log(norm + root) / norm
        inner = jnp.sum(lorentz * later, axis=1, keepdims=True)
        coefficient = (1.0 / root - phi) / (norm * norm)
        dlorentz = phi * later + (coefficient * inner) * lorentz
        td[t, 0] = (phi * lorentz).astype(BF16)
        td[t, 1] = (lift * dlorentz).astype(BF16)
        td_cross().start()
        for i in range(1, NY):
            td_copy(i, 0).start()

    def tangent_pass():
        ref = td.at[(1 - xl) * NY + y]
        remote(ref, ref, asend_sem.at[6], arecv_sem.at[6], flip).wait_recv()
        for i in range(1, NY):
            td_copy(i, 1).start()

    width = gpart.shape[-1]
    half = width // 2

    def g1_copy():
        return remote(gpart.at[1 - c], g1recv, g12send_sem.at[0], g12recv_sem.at[0], sibling)

    def g2_copy():
        return remote(g2send, g2recv, g12send_sem.at[1], g12recv_sem.at[1], partner)

    def g3_copy(i):
        to = (z + i) % NZ
        return remote(
            g3send.at[to], g3recv.at[i - 1], g3send_sem.at[i - 1], g3recv_sem.at[i - 1],
            at(to, h, c),
        )

    def grad_step():
        for side in range(2):
            for i in range(1, NY):
                td_arrival(i, side).wait_recv()
        tangent = td[:, 0].reshape(tokens, 256)
        turned[0] = tangent.T
        turned[1] = td[:, 1].reshape(tokens, 256).T

        def put(value, cols):
            for k in range(32):
                gpart[k % 2, (k // 2) % 2, k // 4, :, cols] = value[k * 8 : (k + 1) * 8]

        def in_tile(n, carry):
            cols = pl.ds(pl.multiple_of(n * 256, 256), 256)
            put(jnp.dot(turned[1], hid[:, cols], preferred_element_type=F32), cols)
            return carry

        lax.fori_loop(0, hid.shape[1] // 256, in_tile, 0)
        for n in range(2):
            cols = slice(n * 256, (n + 1) * 256)
            part = jnp.dot(turned[0], cot[:, cols], preferred_element_type=F32)
            put(adapter_scale * part, slice(hid.shape[1] + n * 256, hid.shape[1] + (n + 1) * 256))
        g1_copy().start()
        for n in range(2):
            adapt[n] = adapter_scale * jnp.dot(
                tangent, aout[:, n * 256 : (n + 1) * 256], preferred_element_type=F32
            )

    def grad_two():
        g1_copy().wait_recv()
        g2send[...] = (gpart[c, 1 - h] + g1recv[1 - h]).reshape(64, width).astype(BF16)
        g2_copy().start()
        gpart[c, h] = gpart[c, h] + g1recv[h]

    def grad_three():
        g2_copy().wait_recv()
        gpart[c, h] = gpart[c, h] + g2recv[...].astype(F32).reshape(NZ, 8, width)
        for k in range(NZ):
            block = gpart[c, h, k]
            g3send[k] = jnp.concatenate([block[:, :half], block[:, half:]], axis=0).astype(BF16)
        for i in range(1, NZ):
            g3_copy(i).start()

    def grad_last():
        block = gpart[c, h, z]
        total = jnp.concatenate([block[:, :half], block[:, half:]], axis=0)
        for i in range(1, NZ):
            g3_copy(i).wait_recv()
            total = total + g3recv[i - 1].astype(F32)
        cut = hid.shape[1] - half
        gin_ref[:, :half] = total[:8]
        gin_ref[:, half:] = total[8:, :cut]
        gout_ref[...] = total[8:, cut:]

    tall = tokens // 2

    def part_copy(p, m):
        zs, hs = place(p)
        to = zs % NY
        idx, src = (zs // NY) * 2 + hs, (y - to + NY - 1) % NY
        rows = pl.ds(m * tall, tall)
        return remote(
            psend.at[p, rows], precv.at[idx, src, rows],
            csend_sem.at[p, m], crecv_sem.at[idx, src, m], (d, xl * NY + to),
        )

    def part_arrival(idx, src, m):
        ref = precv.at[idx, src, pl.ds(m * tall, tall)]
        return remote(ref, ref, csend_sem.at[0, m], crecv_sem.at[idx, src, m], sibling)

    def x_copy(hs, m):
        rows = pl.ds(m * tall, tall)
        return remote(
            xsend.at[hs, rows], xrecv.at[hs, rows], xsend_sem.at[hs, m], xrecv_sem.at[hs, m],
            (d, (1 - xl) * NY + y),
        )

    def reduce_strip(p):
        zs, hs = place(p)
        idx = (zs // NY) * 2 + hs

        @pl.when(zs % NY == y)
        def _():
            keep = zs // NY == xl

            def tile(m, carry):
                for src in range(NY - 1):
                    part_arrival(idx, src, m).wait_recv()
                rows = pl.ds(pl.multiple_of(m * tall, tall), tall)
                value = acc[idx, rows, :]
                for src in range(NY - 1):
                    value = value + precv[idx, src, rows, :].astype(F32)
                acc[idx, rows, :] = value
                xsend[jnp.where(keep, 2, hs), rows, :] = value.astype(BF16)

                @pl.when(jnp.logical_not(keep))
                def _():
                    x_copy(hs, m).start()

                return carry

            lax.fori_loop(0, 2, tile, 0)

    def late(p, carry):
        reduce_strip(p)
        return carry

    phases = ((3, rank_step), (5, tangent_step), (7, tangent_pass)) + (
        (12, grad_step), (14, grad_two), (15, grad_three),
    )

    def step(p, carry):
        zs, hs = place(p)
        for first in groups:

            @pl.when(p == first)
            def _(first=first):
                arrive(first)

        for part in range(2):
            share(p, part, 1 - c).wait_recv()
        to = zs % NY
        slot = jnp.where(to == y, (zs // NY) * 2 + hs, 4)

        right = jnp.concatenate([weights[zs, hs, 0], weights[zs, hs, 1]], axis=1)
        value = jnp.dot(hid[...], right, preferred_element_type=F32)
        for m in range(2):
            cut = slice(m * tall, (m + 1) * tall)
            psend[p, cut, :] = value[cut].astype(BF16)
            acc[slot, cut, :] = value[cut]

        @pl.when(to != y)
        def _():
            for m in range(2):
                part_copy(p, m).start()

        lax.fori_loop(look(p - 1, REDUCED), look(p, REDUCED), late, 0)

        for when, phase in phases:

            @pl.when(p == when)
            def _(phase=phase):
                phase()

        return carry

    lax.fori_loop(0, 16, step, 0)

    lax.fori_loop(REDUCED[-1], 16, late, 0)

    def last(i, carry):
        n, m = i // 2, i % 2
        x_copy(n, m).wait_recv()
        rows = pl.ds(pl.multiple_of(m * tall, tall), tall)
        value = acc[xl * 2 + n, rows, :] + xrecv[n, rows, :].astype(F32) + adapt[n, rows, :]
        out_ref[rows, pl.ds(pl.multiple_of(n * 256, 256), 256)] = value.astype(BF16)
        return carry

    lax.fori_loop(0, 4, last, 0)
    grad_last()

    for q in range(1, 16):
        for part in range(2):
            forward(q, part).wait_send()

    def drain(p, carry):
        zs, hs = place(p)
        for part in range(2):
            share(p, part, c).wait_send()

        @pl.when(zs % NY != y)
        def _():
            for m in range(2):
                part_copy(p, m).wait_send()

        return carry

    lax.fori_loop(0, 16, drain, 0)
    for n in range(2):
        for m in range(2):
            x_copy(n, m).wait_send()
    for i in range(1, NY):
        rank_copy(i).wait_send()
        td_copy(i, 0).wait_send()
        td_copy(i, 1).wait_send()
    rank_cross().wait_send()
    td_cross().wait_send()
    for i in range(1, NZ):
        g3_copy(i).wait_send()
    g1_copy().wait_send()
    g2_copy().wait_send()


def place_results(*refs):
    for i in range(3):
        refs[i + 3][...] = refs[i][...]


def shards(hidden, base_weight, adapter_in, adapter_out, cotangent):
    tokens, ff = hidden.shape
    rank, cols = adapter_out.shape
    features = ff * lax.axis_size("tensor")
    width = ff + cols
    dma = pltpu.SemaphoreType.DMA
    hbm = pl.BlockSpec(memory_space=pl.ANY)
    vmem = pl.BlockSpec(memory_space=pltpu.VMEM)
    results = (
        jax.ShapeDtypeStruct((tokens, cols), BF16),
        jax.ShapeDtypeStruct((8, ff), F32),
        jax.ShapeDtypeStruct((8, cols), F32),
    )
    made = pl.pallas_call(
        functools.partial(kernel, features),
        out_shape=results,
        in_specs=[hbm] * 5,
        out_specs=(vmem,) * 3,
        scratch_shapes=[
            pltpu.VMEM((tokens, ff), BF16),
            pltpu.VMEM((rank, ff), BF16),
            pltpu.VMEM((rank, cols), BF16),
            pltpu.VMEM((tokens, cols), BF16),
            pltpu.VMEM((NZ, 2, 2, ff, 128), BF16),
            pltpu.VMEM((16, tokens, 256), BF16),
            pltpu.VMEM((4, 3, tokens, 256), BF16),
            pltpu.VMEM((5, tokens, 256), F32),
            pltpu.VMEM((3, tokens, 256), BF16),
            pltpu.VMEM((2, tokens, 256), BF16),
            pltpu.VMEM((NY, 2, tokens // NT + 8, 512), F32),
            pltpu.VMEM((NY - 1, 2, tokens // NT + 8, 512), F32),
            pltpu.VMEM((tokens // NT + 8, 512), F32),
            pltpu.VMEM((NT, 2, tokens // NT, rank), BF16),
            pltpu.VMEM((2, rank, tokens), BF16),
            pltpu.VMEM((2, 2, NZ, 8, width), F32),
            pltpu.VMEM((2, NZ, 8, width), F32),
            pltpu.VMEM((NZ * 8, width), BF16),
            pltpu.VMEM((NZ * 8, width), BF16),
            pltpu.VMEM((NZ, 16, width // 2), BF16),
            pltpu.VMEM((NZ - 1, 16, width // 2), BF16),
            pltpu.VMEM((2, tokens, 256), F32),
            dma((5,)),
            dma((16, 2)),
            dma((16, 2)),
            dma((16, 2)),
            dma((16, 2)),
            dma((16, 2)),
            dma((4, 3, 2)),
            dma((2, 2)),
            dma((2, 2)),
            dma((4,)),
            dma((4,)),
            dma((7,)),
            dma((7,)),
            dma((2,)),
            dma((2,)),
            dma((7,)),
            dma((7,)),
        ],
        compiler_params=pltpu.CompilerParams(
            collective_id=0, has_side_effects=True, vmem_limit_bytes=56 << 20
        ),
        name="adapter_step",
    )(hidden, base_weight, adapter_in, adapter_out, cotangent)
    return pl.pallas_call(
        place_results,
        out_shape=results,
        in_specs=[vmem] * 3,
        out_specs=(vmem,) * 3,
        name="place_results",
    )(*made)


def solution(mesh):
    return jax.shard_map(
        shards,
        mesh=mesh,
        in_specs=(
            P("dp", "tensor"),
            P("tensor", "dp"),
            P(None, "tensor"),
            P(None, "tensor"),
            P("dp", "tensor"),
        ),
        out_specs=(P("dp", "tensor"), P("dp", "tensor"), P("dp", "tensor")),
        check_vma=False,
    )
```
